256 devices in a mesh: date: 64 (over z, x, core), space: 4 (over y).
Axes of the slice: x: 4, y: 4, z: 8, core: 2. Of those that a mesh axis runs over, the one named last changes fastest.
Arguments:
- slc: bfloat16 [2, 256, 256, 2048], P(None, 'date', 'space'), may hold values from -6 to 6
- pairs: int32 [384, 2], P('date'), may hold values from 0 to 255, as said below
Outputs:
- coherence: float32 [384, 64, 128], P('date', 'space')
- filtered: float32 [2, 384, 64, 128], P(None, 'date', 'space')
The draws below stay inside these ranges and needn't reach their ends.
Inputs may be any that keep to these rules, and one draw needn't show every extreme that they name: Pairs of rows k * 6 to (k + 1) * 6 - 1 have their reference date among dates k * 4 to (k + 1) * 4 - 1 and a later secondary date below (k + 2) * 4, and below 256; the pairs of one such block are distinct.
All inputs are finite; a program needn't handle non-finite values.
Results may differ from the reference program's by a relative error of at most 0.0003.
Values may be sent and summed in bfloat16 or wider, within the bound.
No kernel may reach another device: no remote copies, remote signals or barrier semaphores. Data moves between devices by JAX's collectives and lax.ppermute only.
A program may use at most 128 MiB of HBM per device.

```python
import jax
import jax.numpy as jnp
import numpy as np
from jax import lax

DATE_DEV = 4
PAIRS_DEV = 6
RG = 2048
DATES = 256
AZ = 256


def draw_pairs(key, part):
    devices = DATES // DATE_DEV
    every = [(r, s) for r in range(DATE_DEV) for s in range(r + 1, 2 * DATE_DEV)]
    inside = [(r, s) for r in range(DATE_DEV) for s in range(r + 1, DATE_DEV)]
    every_table = jnp.asarray(np.array(every, dtype=np.int32))
    inside_table = jnp.asarray(np.array(inside, dtype=np.int32))
    leading = 2 * DATE_DEV - 1
    keys = jax.random.split(key, devices)

    def choose(single):
        first_key, rest_key = jax.random.split(single)
        first_index = jax.random.permutation(first_key, leading)[:1]
        rest_index = leading + jax.random.permutation(rest_key, len(every) - leading)[:PAIRS_DEV - 1]
        return every_table[jnp.concatenate([first_index, rest_index]).astype(jnp.int32)]
    picked = jax.vmap(choose)(keys)
    final = inside_table[jax.random.permutation(jax.random.fold_in(key, 7), len(inside))[:PAIRS_DEV]]
    picked = picked.at[devices - 1].set(final)
    offsets = (jnp.arange(devices, dtype=jnp.int32) * DATE_DEV)[:, None, None]
    return (picked + offsets).reshape(devices * PAIRS_DEV, 2).astype(jnp.int32)


def shard_levels(rng, dims, pieces, low, top_value):
    gain, own = 1.0, jax.random.fold_in(rng, 6)
    for axis_at, parts in pieces:
        steps = jnp.exp(jax.random.uniform(jax.random.fold_in(own, axis_at), (parts,), jnp.float32, low / len(pieces), top_value / len(pieces)))
        gain = gain * jnp.repeat(steps, dims[axis_at] // parts).reshape([-1 if axis == axis_at else 1 for axis in range(len(dims))])
    return gain


def centred(rng, dims, scale, reach, cuts=(), kind=jnp.bfloat16):
    loudness = shard_levels(rng, dims, cuts, -0.22, 0.18) if cuts else 1.0
    values = jax.random.normal(rng, dims, jnp.float32) * scale * loudness
    return jnp.minimum(jnp.maximum(values, -reach), reach).astype(kind)


def setup_inputs(seed: int = 0) -> dict:
    streams_of = jax.random.split(jax.random.key(seed), 3)
    return {
        "slc": centred(streams_of[0], (2, DATES, AZ, RG), 1.0, 6.0, ((1, 64), (2, 4))),
        "pairs": draw_pairs(jax.random.fold_in(streams_of[2], 71), 0),
    }


def pooled(term):
    lead = term.shape[:-2]
    rows, cols = (term.shape[-2], term.shape[-1])
    return lax.optimization_barrier(jnp.mean(term.reshape(lead + (rows // 4, 4, cols // 16, 16)), axis=(-3, -1)))

def multilook(ref, sec):
    ar = ref[0].astype(jnp.float32)
    ai = ref[1].astype(jnp.float32)
    br = sec[0].astype(jnp.float32)
    bi = sec[1].astype(jnp.float32)
    return jnp.stack([pooled(ar * br + ai * bi), pooled(ai * br - ar * bi), pooled(ar * ar + ai * ai), pooled(br * br + bi * bi)])

def normalize(looks):
    scale = 1.0 / jnp.sqrt((looks[2] + 1e-06) * (looks[3] + 1e-06))
    g_re = looks[0] * scale
    g_im = looks[1] * scale
    return (g_re, g_im, jnp.sqrt(g_re * g_re + g_im * g_im))

def tables():
    index = jnp.arange(32, dtype=jnp.float32)
    phase = 2.0 * jnp.pi * index[:, None] * index[None, :] / 32.0
    taper = jnp.where(index < 16, (index + 0.5) / 16.0, (31.5 - index) / 16.0)
    return (jnp.cos(phase), jnp.sin(phase), taper)

def patches(field):
    count, rows, cols = field.shape
    blocks = field.reshape(count, rows // 16, 16, cols // 16, 16)
    blocks = jnp.concatenate([blocks[:, :-1], blocks[:, 1:]], axis=2)
    blocks = jnp.concatenate([blocks[:, :, :, :-1], blocks[:, :, :, 1:]], axis=4)
    return blocks

def assemble(blocks):
    first, second = (blocks[:, :, :16], blocks[:, :, 16:])
    blocks = jnp.pad(first, ((0, 0), (0, 1), (0, 0), (0, 0), (0, 0))) + jnp.pad(second, ((0, 0), (1, 0), (0, 0), (0, 0), (0, 0)))
    first, second = (blocks[..., :16], blocks[..., 16:])
    blocks = jnp.pad(first, ((0, 0), (0, 0), (0, 0), (0, 1), (0, 0))) + jnp.pad(second, ((0, 0), (0, 0), (0, 0), (1, 0), (0, 0)))
    count, nrow, _, ncol, _ = blocks.shape
    return blocks.reshape(count, nrow * 16, ncol * 16)[:, 16:-16, 16:-16]

def transform(xr, xi, cosine, sine, sign):
    high = lax.Precision.HIGHEST
    ur = jnp.einsum('ka,abn->kbn', cosine, xr, precision=high) + sign * jnp.einsum('ka,abn->kbn', sine, xi, precision=high)
    ui = jnp.einsum('ka,abn->kbn', cosine, xi, precision=high) - sign * jnp.einsum('ka,abn->kbn', sine, xr, precision=high)
    zr = jnp.einsum('lb,kbn->kln', cosine, ur, precision=high) + sign * jnp.einsum('lb,kbn->kln', sine, ui, precision=high)
    zi = jnp.einsum('lb,kbn->kln', cosine, ui, precision=high) - sign * jnp.einsum('lb,kbn->kln', sine, ur, precision=high)
    return (zr, zi)

def goldstein(field):
    cosine, sine, taper = tables()
    padded = jnp.pad(field, ((0, 0), (0, 0), (0, 0), (16, 16)))
    pieces_re = patches(padded[0])
    pieces_im = patches(padded[1])
    count, nrow, _, ncol, _ = pieces_re.shape
    xr = pieces_re.transpose(2, 4, 0, 1, 3).reshape(32, 32, -1)
    xi = pieces_im.transpose(2, 4, 0, 1, 3).reshape(32, 32, -1)
    zr, zi = transform(xr, xi, cosine, sine, 1.0)
    power = zr * zr + zi * zi
    smooth = jnp.zeros_like(power)
    for shift_k in (-1, 0, 1):
        for shift_l in (-1, 0, 1):
            smooth = smooth + jnp.roll(power, (shift_k, shift_l), axis=(0, 1))
    weight = (smooth / 9.0 + 1e-06) ** 0.25
    yr, yi = transform(zr * weight, zi * weight, cosine, sine, -1.0)
    window = (taper[:, None] * taper[None, :])[:, :, None] / 1024.0
    yr = (yr * window).reshape(32, 32, count, nrow, ncol).transpose(2, 3, 0, 4, 1)
    yi = (yi * window).reshape(32, 32, count, nrow, ncol).transpose(2, 3, 0, 4, 1)
    return jnp.stack([assemble(yr), assemble(yi)])

def reference(slc, pairs):

    def one_pair(pair):
        ref = lax.dynamic_index_in_dim(slc, pair[0].astype(jnp.int32), 1, keepdims=False)
        sec = lax.dynamic_index_in_dim(slc, pair[1].astype(jnp.int32), 1, keepdims=False)
        return multilook(ref, sec)
    looks = lax.map(one_pair, pairs).transpose(1, 0, 2, 3)
    g_re, g_im, coherence = normalize(looks)
    field = jnp.pad(jnp.stack([g_re, g_im]), ((0, 0), (0, 0), (16, 16), (0, 0)))
    return (coherence, goldstein(field))
```

```python
import functools

import jax
import jax.numpy as jnp
import numpy as np
from jax import lax
from jax.experimental import pallas as pl
from jax.experimental.pallas import tpu as pltpu
from jax.sharding import PartitionSpec as P

F32, BF16 = jnp.float32, jnp.bfloat16
PATCHES = 9
LANES = 384


def split(value):
    high = value.astype(BF16)
    return high, (value - high.astype(F32)).astype(BF16)


def split_table(table):
    high = table.astype(np.float32).astype(jnp.bfloat16)
    low = (table - high.astype(np.float64)).astype(np.float32).astype(jnp.bfloat16)
    return high, low


@functools.cache
def filter_tables():
    index = np.arange(32)
    phase = 2.0 * np.pi * np.outer(index, index) / 32.0
    cosine, sine = np.cos(phase), np.sin(phase)
    taper = np.where(index < 16, (index + 0.5) / 16.0, (31.5 - index) / 16.0)
    rows = np.zeros((2, 2, 32, 2, 48))
    for j in range(2):
        at = slice(16 * j, 16 * j + 32)
        rows[0, j, :, 0, at], rows[0, j, :, 1, at] = cosine, sine
        rows[1, j, :, 0, at], rows[1, j, :, 1, at] = -sine, cosine
    rows = rows.reshape(128, 96)
    columns = np.zeros((2, 128, 2, LANES))
    back = np.zeros((2, LANES, 2, 128))
    for c in range(PATCHES):
        for b in range(32):
            column = 16 * c - 16 + b
            if not 0 <= column < 128:
                continue
            at = slice(32 * c, 32 * c + 32)
            columns[0, column, 0, at], columns[1, column, 0, at] = cosine[:, b], sine[:, b]
            columns[0, column, 1, at], columns[1, column, 1, at] = -sine[:, b], cosine[:, b]
            scale = taper[b] / 32.0
            back[0, at, 0, column], back[1, at, 0, column] = cosine[:, b] * scale, -sine[:, b] * scale
            back[0, at, 1, column], back[1, at, 1, column] = sine[:, b] * scale, cosine[:, b] * scale
    columns = columns.reshape(256, 2 * LANES)
    back = back.reshape(2 * LANES, 256)
    final = np.zeros((2, 16, 2, 2, 32))
    for j in range(2):
        for row in range(16):
            a = row + 16 * (1 - j)
            scale = taper[a] / 32.0
            final[0, row, 0, j], final[0, row, 1, j] = cosine[:, a] * scale, -sine[:, a] * scale
            final[1, row, 0, j], final[1, row, 1, j] = sine[:, a] * scale, cosine[:, a] * scale
    final = final.reshape(32, 128)
    rows_high, rows_low = split_table(rows)
    final_high, final_low = split_table(final)
    return (
        np.concatenate([rows_high, rows_high, rows_low], axis=1),
        *split_table(columns),
        *split_table(back),
        np.concatenate([final_high, final_high, final_low], axis=1),
    )


def looks_kernel(pairs_ref, own_ref, next_ref, gamma_ref, coherence_ref, images, terms, total, power):
    chunks = own_ref.shape[-1] // 256
    count = pairs_ref.shape[0]
    half = terms.shape[1] // 2
    for c in range(chunks):
        slot = c % 2
        for date in range(4):
            for part in range(2):
                for side in range(2):
                    at = pl.ds(256 * c + 128 * side, 128)
                    images[slot, date, part, side] = own_ref[part, date, :, at].astype(F32)
                    images[slot, 4 + date, part, side] = next_ref[part, date, :, at].astype(F32)

        def load(date, part, side, phase):
            return images[slot, date, part, side, pl.ds(phase, 16, stride=4), :]

        def keep(index, side, value):
            high, low = split(value)
            at = pl.ds(128 * side, 128)
            terms[slot, pl.ds(16 * index, 16), at] = high
            terms[slot, pl.ds(half + 16 * index, 16), at] = low

        for p in range(count):
            first, second = pairs_ref[p, 0], pairs_ref[p, 1]
            for side in range(2):
                re = im = None
                for phase in range(4):
                    ar, ai = load(first, 0, side, phase), load(first, 1, side, phase)
                    br, bi = load(second, 0, side, phase), load(second, 1, side, phase)
                    one, other = ar * br + ai * bi, ai * br - ar * bi
                    re, im = (one, other) if re is None else (re + one, im + other)
                keep(p, side, re)
                keep(count + p, side, im)
        for date in range(8):
            for side in range(2):
                square = None
                for phase in range(4):
                    re, im = load(date, 0, side, phase), load(date, 1, side, phase)
                    one = re * re + im * im
                    square = one if square is None else square + one
                keep(2 * count + date, side, square)
        sample = lax.broadcasted_iota(jnp.int32, (256, 128), 0)
        column = lax.broadcasted_iota(jnp.int32, (256, 128), 1)
        pool = ((sample >> 4) + 16 * c == column).astype(F32).astype(BF16)
        part = jnp.dot(terms[slot], pool, preferred_element_type=F32)
        total[...] = part if c == 0 else total[...] + part
    power[...] = (
        total[pl.ds(32 * count, 128)] + total[pl.ds(half + 32 * count, 128)]
    ).reshape(8, 16, 128) * (1.0 / 64.0)
    for p in range(count):
        first, second = pairs_ref[p, 0], pairs_ref[p, 1]
        scale = lax.rsqrt((power[first] + 1e-6) * (power[second] + 1e-6)) * (1.0 / 64.0)
        re = (total[pl.ds(16 * p, 16)] + total[pl.ds(half + 16 * p, 16)]) * scale
        at = 16 * (count + p)
        im = (total[pl.ds(at, 16)] + total[pl.ds(half + at, 16)]) * scale
        gamma_ref[0, p] = re
        gamma_ref[1, p] = im
        coherence_ref[p] = jnp.sqrt(re * re + im * im)


def looks(pairs, own, following):
    count = pairs.shape[0]
    rows = 16 * (2 * count + 8)
    vmem = pl.BlockSpec(memory_space=pltpu.VMEM)
    return pl.pallas_call(
        looks_kernel,
        out_shape=(
            jax.ShapeDtypeStruct((2, count, 16, 128), F32),
            jax.ShapeDtypeStruct((count, 16, 128), F32),
        ),
        in_specs=[pl.BlockSpec(memory_space=pltpu.SMEM), vmem, vmem],
        out_specs=(vmem, vmem),
        scratch_shapes=[
            pltpu.VMEM((2, 8, 2, 2, 64, 128), F32),
            pltpu.VMEM((2, 2 * rows, 256), BF16),
            pltpu.VMEM((2 * rows, 128), F32),
            pltpu.VMEM((8, 16, 128), F32),
        ],
        compiler_params=pltpu.CompilerParams(vmem_limit_bytes=32 << 20),
        name="looks",
    )(pairs, own, following)


def ring(power, axis, step, index):
    size = power.shape[axis]
    near = pltpu.roll(power, 1 if step > 0 else size - 1, axis)
    wrap = pltpu.roll(power, size - 31 if step > 0 else 31, axis)
    return jnp.where(index == (0 if step > 0 else 31), wrap, near)


def filter_kernel(
    low_ref, own_ref, high_ref, rows_ref, columns_high, columns_low, back_high, back_low,
    final_ref, out_ref, field, spectra, weighted, result,
):
    count = own_ref.shape[1]
    for p in range(count):
        lanes = pl.ds(128 * p, 128)
        for part in range(2):
            for k, ref in enumerate((low_ref, own_ref, high_ref)):
                high, low = split(ref[part, p])
                at = 48 * part + 16 * k
                field[pl.ds(at, 16), lanes] = high
                field[pl.ds(96 + at, 16), lanes] = low
                field[pl.ds(192 + at, 16), lanes] = high
    along = jnp.dot(rows_ref[...], field[...], preferred_element_type=F32)
    for p in range(count):
        for part in range(2):
            high, low = split(along[64 * part : 64 * part + 64, 128 * p : 128 * p + 128])
            spectra[0, pl.ds(64 * p, 64), pl.ds(128 * part, 128)] = high
            spectra[1, pl.ds(64 * p, 64), pl.ds(128 * part, 128)] = low
    lane = lax.broadcasted_iota(jnp.int32, (64, 128), 1) & 31
    line = lax.broadcasted_iota(jnp.int32, (64, 128), 0) & 31
    for block in range(LANES // 128):
        parts = []
        for part in range(2):
            at = pl.ds(LANES * part + 128 * block, 128)
            parts.append(
                jnp.dot(spectra[0], columns_high[:, at], preferred_element_type=F32)
                + jnp.dot(spectra[1], columns_high[:, at], preferred_element_type=F32)
                + jnp.dot(spectra[0], columns_low[:, at], preferred_element_type=F32)
            )
        for p in range(count):
            re, im = (value[64 * p : 64 * p + 64] for value in parts)
            power = re * re + im * im
            power = power + ring(power, 1, 1, lane) + ring(power, 1, -1, lane)
            power = power + ring(power, 0, 1, line) + ring(power, 0, -1, line)
            weight = lax.rsqrt(lax.rsqrt(power * (1.0 / 9.0) + 1e-6))
            for part, value in enumerate((re, im)):
                high, low = split(value * weight)
                at = pl.ds(LANES * part + 128 * block, 128)
                weighted[0, pl.ds(64 * p, 64), at] = high
                weighted[1, pl.ds(64 * p, 64), at] = low
    across = (
        jnp.dot(weighted[0], back_high[...], preferred_element_type=F32)
        + jnp.dot(weighted[1], back_high[...], preferred_element_type=F32)
        + jnp.dot(weighted[0], back_low[...], preferred_element_type=F32)
    )
    for p in range(count):
        lanes = pl.ds(128 * p, 128)
        for part in range(2):
            high, low = split(across[64 * p : 64 * p + 64, 128 * part : 128 * part + 128])
            at = 64 * part
            result[pl.ds(at, 64), lanes] = high
            result[pl.ds(128 + at, 64), lanes] = low
            result[pl.ds(256 + at, 64), lanes] = high
    out = jnp.dot(final_ref[...], result[...], preferred_element_type=F32)
    for p in range(count):
        for part in range(2):
            out_ref[part, p] = out[16 * part : 16 * part + 16, 128 * p : 128 * p + 128]


def goldstein(low, own, high):
    count = own.shape[1]
    vmem = pl.BlockSpec(memory_space=pltpu.VMEM)
    tables = [jnp.asarray(table) for table in filter_tables()]
    return pl.pallas_call(
        filter_kernel,
        out_shape=jax.ShapeDtypeStruct((2, count, 16, 128), F32),
        in_specs=[vmem] * 9,
        out_specs=vmem,
        scratch_shapes=[
            pltpu.VMEM((288, 128 * count), BF16),
            pltpu.VMEM((2, 64 * count, 256), BF16),
            pltpu.VMEM((2, 64 * count, 2 * LANES), BF16),
            pltpu.VMEM((384, 128 * count), BF16),
        ],
        compiler_params=pltpu.CompilerParams(vmem_limit_bytes=32 << 20),
        name="goldstein",
    )(low, own, high, *tables)


def per_device(slc, pairs):
    dates = lax.axis_size("date")
    strips = lax.axis_size("space")
    local_pairs = pairs - lax.axis_index("date") * slc.shape[1]
    following = lax.ppermute(slc, "date", [(i + 1, i) for i in range(dates - 1)])
    gamma, coherence = looks(local_pairs, slc, following)
    low = lax.ppermute(gamma, "space", [(i, i + 1) for i in range(strips - 1)])
    high = lax.ppermute(gamma, "space", [(i + 1, i) for i in range(strips - 1)])
    return coherence, goldstein(low, gamma, high)


def solution(mesh):
    return jax.shard_map(
        per_device,
        mesh=mesh,
        in_specs=(P(None, "date", "space", None), P("date", None)),
        out_specs=(P("date", "space", None), P(None, "date", "space", None)),
        check_vma=False,
    )
```

```python
import functools

import jax
import jax.numpy as jnp
import numpy as np
from jax import lax
from jax.experimental import pallas as pl
from jax.experimental.pallas import tpu as pltpu
from jax.sharding import PartitionSpec as P

F32, BF16 = jnp.float32, jnp.bfloat16
PATCHES, BLOCKS = 9, 3


def split(value):
    high = value.astype(BF16)
    return high, (value - high.astype(F32)).astype(BF16)


def split_table(table):
    high = table.astype(np.float32).astype(jnp.bfloat16)
    low = (table - high.astype(np.float64)).astype(np.float32).astype(jnp.bfloat16)
    return high, low


@functools.cache
def filter_tables():
    index = np.arange(32)
    phase = 2.0 * np.pi * np.outer(index, index) / 32.0
    cosine, sine = np.cos(phase), np.sin(phase)
    taper = np.where(index < 16, (index + 0.5) / 16.0, (31.5 - index) / 16.0)
    rows = np.zeros((2, 2, 32, 2, 48))
    final = np.zeros((2, 16, 2, 2, 32))
    for j in range(2):
        at = slice(16 * j, 16 * j + 32)
        rows[0, j, :, 0, at], rows[0, j, :, 1, at] = cosine, sine
        rows[1, j, :, 0, at], rows[1, j, :, 1, at] = -sine, cosine
        for row in range(16):
            a = row + 16 * (1 - j)
            scale = taper[a] / 32.0
            final[0, row, 0, j], final[0, row, 1, j] = cosine[:, a] * scale, -sine[:, a] * scale
            final[1, row, 0, j], final[1, row, 1, j] = sine[:, a] * scale, cosine[:, a] * scale
    rows_high, rows_low = split_table(rows.reshape(128, 96))
    final_high, final_low = split_table(final.reshape(32, 128))
    lane = np.arange(128)
    place = (np.arange(32)[:, None] + 16 - 16 * (lane // 32)[None]) % 32
    fore = 2.0 * np.pi * place * (lane % 32)[None] / 32.0
    place = (lane[None] + 16 - 16 * (lane // 32)[:, None]) % 32
    back = 2.0 * np.pi * place * (lane % 32)[:, None] / 32.0
    scale = taper[place] / 32.0
    return (
        np.concatenate([rows_high, rows_high, rows_low], axis=1),
        np.concatenate([final_high, final_high, final_low], axis=1),
        np.stack([*split_table(np.cos(fore)), *split_table(np.sin(fore))]),
        np.stack([*split_table(np.cos(back) * scale), *split_table(np.sin(back) * scale)]),
    )


def looks_kernel(pairs_ref, own_ref, next_ref, *refs, start, added, coherence):
    extra, refs = refs[:added], refs[added:]
    gamma_ref, refs = refs[0], refs[1:]
    if coherence:
        coherence_ref, refs = refs[0], refs[1:]
    images, terms, total, power = refs
    chunks = own_ref.shape[-1] // 256
    count = pairs_ref.shape[0]
    half = terms.shape[1] // 2
    for c in range(chunks):
        slot = c % 2
        for date in range(4):
            for part in range(2):
                for side in range(2):
                    at = pl.ds(256 * c + 128 * side, 128)
                    images[slot, date, part, side] = own_ref[part, date, :, at].astype(F32)
                    images[slot, 4 + date, part, side] = next_ref[part, date, :, at].astype(F32)

        def load(date, part, side, phase):
            return images[slot, date, part, side, pl.ds(phase, 16, stride=4), :]

        def keep(index, side, value):
            high, low = split(value)
            at = pl.ds(128 * side, 128)
            terms[slot, pl.ds(16 * index, 16), at] = high
            terms[slot, pl.ds(half + 16 * index, 16), at] = low

        for p in range(count):
            first, second = pairs_ref[p, 0], pairs_ref[p, 1]
            for side in range(2):
                re = im = None
                for phase in range(4):
                    ar, ai = load(first, 0, side, phase), load(first, 1, side, phase)
                    br, bi = load(second, 0, side, phase), load(second, 1, side, phase)
                    one, other = ar * br + ai * bi, ai * br - ar * bi
                    re, im = (one, other) if re is None else (re + one, im + other)
                keep(p, side, re)
                keep(count + p, side, im)
        for date in range(8):
            for side in range(2):
                square = None
                for phase in range(4):
                    re, im = load(date, 0, side, phase), load(date, 1, side, phase)
                    one = re * re + im * im
                    square = one if square is None else square + one
                keep(2 * count + date, side, square)
        sample = lax.broadcasted_iota(jnp.int32, (256, 128), 0)
        column = lax.broadcasted_iota(jnp.int32, (256, 128), 1)
        pool = ((sample >> 4) + (start // 16 + 16 * c) == column).astype(F32).astype(BF16)
        part = jnp.dot(terms[slot], pool, preferred_element_type=F32)
        total[...] = part if c == 0 else total[...] + part
    power[...] = (
        total[pl.ds(32 * count, 128)] + total[pl.ds(half + 32 * count, 128)]
    ).reshape(8, 16, 128) * (1.0 / 64.0)
    for p in range(count):
        first, second = pairs_ref[p, 0], pairs_ref[p, 1]
        scale = lax.rsqrt((power[first] + 1e-6) * (power[second] + 1e-6)) * (1.0 / 64.0)
        re = (total[pl.ds(16 * p, 16)] + total[pl.ds(half + 16 * p, 16)]) * scale
        at = 16 * (count + p)
        im = (total[pl.ds(at, 16)] + total[pl.ds(half + at, 16)]) * scale
        for ref in extra:
            re, im = re + ref[0, p], im + ref[1, p]
        gamma_ref[0, p] = re
        gamma_ref[1, p] = im
        if coherence:
            coherence_ref[p] = jnp.sqrt(re * re + im * im)


def looks(pairs, own, following, start, extra=(), coherence=False, name="looks"):
    count = pairs.shape[0]
    rows = 16 * (2 * count + 8)
    vmem = pl.BlockSpec(memory_space=pltpu.VMEM)
    shapes = [jax.ShapeDtypeStruct((2, count, 16, 128), F32)]
    if coherence:
        shapes.append(jax.ShapeDtypeStruct((count, 16, 128), F32))
    return pl.pallas_call(
        functools.partial(looks_kernel, start=start, added=len(extra), coherence=coherence),
        out_shape=shapes,
        in_specs=[pl.BlockSpec(memory_space=pltpu.SMEM)] + [vmem] * (2 + len(extra)),
        out_specs=[vmem] * len(shapes),
        scratch_shapes=[
            pltpu.VMEM((2, 8, 2, 2, 64, 128), F32),
            pltpu.VMEM((2, 2 * rows, 256), BF16),
            pltpu.VMEM((2 * rows, 128), F32),
            pltpu.VMEM((8, 16, 128), F32),
        ],
        compiler_params=pltpu.CompilerParams(vmem_limit_bytes=12 << 20),
        name=name,
    )(pairs, own, following, *extra)


def ring(power, axis, step, index):
    size = power.shape[axis]
    near = pltpu.roll(power, 1 if step > 0 else size - 1, axis)
    wrap = pltpu.roll(power, size - 31 if step > 0 else 31, axis)
    return jnp.where(index == (0 if step > 0 else 31), wrap, near)


def filter_kernel(
    odd_ref, near_ref, own_ref, far_ref, rows_ref, final_ref, fore_ref, back_ref,
    out_ref, field, spectra, weighted, result, fore, back,
):
    count = own_ref.shape[1]
    odd = 32 * odd_ref[0]
    for p in range(count):
        lanes = pl.ds(128 * p, 128)
        for part in range(2):
            for place, ref in ((32 - odd, near_ref), (16, own_ref), (odd, far_ref)):
                high, low = split(ref[part, p])
                at = pl.multiple_of(48 * part + place, 16)
                field[pl.ds(at, 16), lanes] = high
                field[pl.ds(96 + at, 16), lanes] = low
                field[pl.ds(192 + at, 16), lanes] = high
    across = lax.broadcasted_iota(jnp.int32, (128, 128), 0)
    along = lax.broadcasted_iota(jnp.int32, (128, 128), 1)
    for level in range(2):
        cosine = jnp.concatenate([fore_ref[level].astype(F32)] * 4, axis=0)
        sine = jnp.concatenate([fore_ref[2 + level].astype(F32)] * 4, axis=0)
        for block in range(BLOCKS):
            patch = 4 * block + (along >> 5) - (across >> 4)
            inside = (patch >= 0) & (patch <= 1) & (4 * block + (along >> 5) < PATCHES)
            cos, sin = (jnp.where(inside, value, 0.0) for value in (cosine, sine))
            at = 256 * block
            fore[level, pl.ds(0, 128), pl.ds(at, 128)] = cos.astype(BF16)
            fore[level, pl.ds(128, 128), pl.ds(at, 128)] = sin.astype(BF16)
            fore[level, pl.ds(0, 128), pl.ds(at + 128, 128)] = (-sin).astype(BF16)
            fore[level, pl.ds(128, 128), pl.ds(at + 128, 128)] = cos.astype(BF16)
    column = jnp.dot(rows_ref[...], field[...], preferred_element_type=F32)
    for p in range(count):
        for part in range(2):
            high, low = split(column[64 * part : 64 * part + 64, 128 * p : 128 * p + 128])
            spectra[0, pl.ds(64 * p, 64), pl.ds(128 * part, 128)] = high
            spectra[1, pl.ds(64 * p, 64), pl.ds(128 * part, 128)] = low
    for level in range(2):
        cosine, sine = back_ref[level].astype(F32), back_ref[2 + level].astype(F32)
        for block in range(BLOCKS):
            patch = 4 * block + (across >> 5) - (along >> 4)
            inside = (patch >= 0) & (patch <= 1) & (4 * block + (across >> 5) < PATCHES)
            cos, sin = (jnp.where(inside, value, 0.0) for value in (cosine, sine))
            at = 256 * block
            back[level, pl.ds(at, 128), pl.ds(0, 128)] = cos.astype(BF16)
            back[level, pl.ds(at, 128), pl.ds(128, 128)] = sin.astype(BF16)
            back[level, pl.ds(at + 128, 128), pl.ds(0, 128)] = (-sin).astype(BF16)
            back[level, pl.ds(at + 128, 128), pl.ds(128, 128)] = cos.astype(BF16)
    lane = lax.broadcasted_iota(jnp.int32, (64, 128), 1) & 31
    line = lax.broadcasted_iota(jnp.int32, (64, 128), 0) & 31
    for block in range(BLOCKS):
        at = pl.ds(256 * block, 256)
        both = (
            jnp.dot(spectra[0], fore[0, :, at], preferred_element_type=F32)
            + jnp.dot(spectra[1], fore[0, :, at], preferred_element_type=F32)
            + jnp.dot(spectra[0], fore[1, :, at], preferred_element_type=F32)
        )
        for p in range(count):
            re, im = both[64 * p : 64 * p + 64, :128], both[64 * p : 64 * p + 64, 128:]
            power = re * re + im * im
            power = power + ring(power, 1, 1, lane) + ring(power, 1, -1, lane)
            power = power + ring(power, 0, 1, line) + ring(power, 0, -1, line)
            weight = lax.rsqrt(lax.rsqrt(power * (1.0 / 9.0) + 1e-6))
            for part, value in enumerate((re, im)):
                high, low = split(value * weight)
                at = pl.ds(256 * block + 128 * part, 128)
                weighted[0, pl.ds(64 * p, 64), at] = high
                weighted[1, pl.ds(64 * p, 64), at] = low
    filtered = (
        jnp.dot(weighted[0], back[0], preferred_element_type=F32)
        + jnp.dot(weighted[1], back[0], preferred_element_type=F32)
        + jnp.dot(weighted[0], back[1], preferred_element_type=F32)
    )
    for p in range(count):
        lanes = pl.ds(128 * p, 128)
        for part in range(2):
            high, low = split(filtered[64 * p : 64 * p + 64, 128 * part : 128 * part + 128])
            at = 64 * part
            result[pl.ds(at, 64), lanes] = high
            result[pl.ds(128 + at, 64), lanes] = low
            result[pl.ds(256 + at, 64), lanes] = high
    out = jnp.dot(final_ref[...], result[...], preferred_element_type=F32)
    for p in range(count):
        for part in range(2):
            out_ref[part, p] = out[16 * part : 16 * part + 16, 128 * p : 128 * p + 128]


def goldstein(odd, near, own, far):
    count = own.shape[1]
    vmem = pl.BlockSpec(memory_space=pltpu.VMEM)
    tables = [jnp.asarray(table) for table in filter_tables()]
    return pl.pallas_call(
        filter_kernel,
        out_shape=jax.ShapeDtypeStruct((2, count, 16, 128), F32),
        in_specs=[pl.BlockSpec(memory_space=pltpu.SMEM)] + [vmem] * (3 + len(tables)),
        out_specs=vmem,
        scratch_shapes=[
            pltpu.VMEM((288, 128 * count), BF16),
            pltpu.VMEM((2, 64 * count, 256), BF16),
            pltpu.VMEM((2, 64 * count, 256 * BLOCKS), BF16),
            pltpu.VMEM((384, 128 * count), BF16),
            pltpu.VMEM((2, 256, 256 * BLOCKS), BF16),
            pltpu.VMEM((2, 256 * BLOCKS, 256), BF16),
        ],
        compiler_params=pltpu.CompilerParams(vmem_limit_bytes=16 << 20),
        name="goldstein",
    )(odd, near, own, far, *tables)


def shifted(value, axis, step):
    size = lax.axis_size(axis)
    return lax.ppermute(value, axis, [(i, (i + step) % size) for i in range(size)])


def swapped(value, axis, first):
    size = lax.axis_size(axis)
    pairs = [(i, i + 1) for i in range(first, size - 1, 2)]
    return lax.ppermute(value, axis, pairs + [(j, i) for i, j in pairs])


COLUMNS = (768, 512, 256)


def per_device(slc, pairs):
    dates = slc.shape[1]
    block = lax.axis_index("date")
    here = pairs - block * dates
    edge = sum(COLUMNS)
    own_last = slc[..., edge:]
    previous_last = shifted(own_last, "date", 1)
    own, following, starts, at = [], [], [], 0
    for width in COLUMNS:
        own.append(slc[..., at : at + width])
        following.append(shifted(own[-1], "date", -1))
        starts.append(at)
        at += width
    there = shifted(here, "date", 1)
    [returned] = looks(there, previous_last, own_last, edge, name="looks_last")
    returned = shifted(returned, "date", -1)
    parts = []
    for k in range(len(COLUMNS) - 1):
        parts += looks(here, own[k], following[k], starts[k], name="looks_part")
    gamma, coherence = looks(
        here, own[-1], following[-1], starts[-1], (*parts, returned), True, name="looks_end"
    )
    near = swapped(gamma, "space", 0)
    far = swapped(gamma, "space", 1)
    odd = (lax.axis_index("space") % 2).astype(jnp.int32).reshape(1)
    return coherence, goldstein(odd, near, gamma, far)


def solution(mesh):
    return jax.shard_map(
        per_device,
        mesh=mesh,
        in_specs=(P(None, "date", "space", None), P("date", None)),
        out_specs=(P("date", "space", None), P(None, "date", "space", None)),
        check_vma=False,
    )
```

```python
import functools

import jax
import jax.numpy as jnp
import numpy as np
from jax import lax
from jax.experimental import pallas as pl
from jax.experimental.pallas import tpu as pltpu
from jax.sharding import PartitionSpec as P

F32, BF16 = jnp.float32, jnp.bfloat16
PATCHES, BLOCKS = 9, 3


def split(value):
    high = value.astype(BF16)
    return high, (value - high.astype(F32)).astype(BF16)


def split_table(table):
    high = table.astype(np.float32).astype(jnp.bfloat16)
    low = (table - high.astype(np.float64)).astype(np.float32).astype(jnp.bfloat16)
    return high, low


@functools.cache
def filter_tables():
    index = np.arange(32)
    phase = 2.0 * np.pi * np.outer(index, index) / 32.0
    cosine, sine = np.cos(phase), np.sin(phase)
    taper = np.where(index < 16, (index + 0.5) / 16.0, (31.5 - index) / 16.0)
    rows = np.zeros((2, 2, 32, 2, 48))
    final = np.zeros((2, 16, 2, 2, 32))
    for j in range(2):
        at = slice(16 * j, 16 * j + 32)
        rows[0, j, :, 0, at], rows[0, j, :, 1, at] = cosine, sine
        rows[1, j, :, 0, at], rows[1, j, :, 1, at] = -sine, cosine
        for row in range(16):
            a = row + 16 * (1 - j)
            scale = taper[a] / 32.0
            final[0, row, 0, j], final[0, row, 1, j] = cosine[:, a] * scale, -sine[:, a] * scale
            final[1, row, 0, j], final[1, row, 1, j] = sine[:, a] * scale, cosine[:, a] * scale
    rows_high, rows_low = split_table(rows.reshape(128, 96))
    final_high, final_low = split_table(final.reshape(32, 128))
    lane = np.arange(128)
    place = (np.arange(32)[:, None] + 16 - 16 * (lane // 32)[None]) % 32
    fore = 2.0 * np.pi * place * (lane % 32)[None] / 32.0
    place = (lane[None] + 16 - 16 * (lane // 32)[:, None]) % 32
    back = 2.0 * np.pi * place * (lane % 32)[:, None] / 32.0
    scale = taper[place] / 32.0
    return (
        np.concatenate([rows_high, rows_high, rows_low], axis=1),
        np.concatenate([final_high, final_high, final_low], axis=1),
        np.stack([*split_table(np.cos(fore)), *split_table(np.sin(fore))]),
        np.stack([*split_table(np.cos(back) * scale), *split_table(np.sin(back) * scale)]),
    )


def pool_terms(pairs_ref, own_ref, next_ref, start, images, terms, total):
    count = pairs_ref.shape[0]
    half = terms.shape[1] // 2
    for c in range(own_ref.shape[-1] // 256):
        slot = c % 2
        for date in range(4):
            for part in range(2):
                for side in range(2):
                    at = pl.ds(256 * c + 128 * side, 128)
                    images[slot, date, part, side] = own_ref[part, date, :, at].astype(F32)
                    images[slot, 4 + date, part, side] = next_ref[part, date, :, at].astype(F32)

        def load(date, part, side, phase):
            return images[slot, date, part, side, pl.ds(phase, 16, stride=4), :]

        def keep(index, side, value):
            high, low = split(value)
            at = pl.ds(128 * side, 128)
            terms[slot, pl.ds(16 * index, 16), at] = high
            terms[slot, pl.ds(half + 16 * index, 16), at] = low

        for p in range(count):
            first, second = pairs_ref[p, 0], pairs_ref[p, 1]
            for side in range(2):
                re = im = None
                for phase in range(4):
                    ar, ai = load(first, 0, side, phase), load(first, 1, side, phase)
                    br, bi = load(second, 0, side, phase), load(second, 1, side, phase)
                    one, other = ar * br + ai * bi, ai * br - ar * bi
                    re, im = (one, other) if re is None else (re + one, im + other)
                keep(p, side, re)
                keep(count + p, side, im)
        for date in range(8):
            for side in range(2):
                square = None
                for phase in range(4):
                    re, im = load(date, 0, side, phase), load(date, 1, side, phase)
                    one = re * re + im * im
                    square = one if square is None else square + one
                keep(2 * count + date, side, square)
        sample = lax.broadcasted_iota(jnp.int32, (256, 128), 0)
        column = lax.broadcasted_iota(jnp.int32, (256, 128), 1)
        pool = ((sample >> 4) + (start // 16 + 16 * c) == column).astype(F32).astype(BF16)
        total[...] += jnp.dot(terms[slot], pool, preferred_element_type=F32)


def fetch(sources, targets, sems):
    return [
        pltpu.make_async_copy(source, target, sems.at[i])
        for i, (source, target) in enumerate(zip(sources, targets))
    ]


def looks_kernel(*refs, start, tables, added, final):
    take = iter(refs)
    pairs_ref, own_ref, next_ref = (next(take) for _ in range(3))
    flag_ref, last_ref = (next(take), next(take)) if final else (None, None)
    extra = [next(take) for _ in range(added)]
    sources = [next(take) for _ in range(tables)]
    gamma_ref = next(take)
    coherence_ref = next(take) if final else None
    targets = [next(take) for _ in range(tables)]
    images, terms, total, power = (next(take) for _ in range(4))
    copies = fetch(sources, targets, next(take)) if tables else []
    for copy in copies:
        copy.start()
    count = pairs_ref.shape[0]
    half = terms.shape[1] // 2
    total[...] = jnp.zeros_like(total)
    pool_terms(pairs_ref, own_ref, next_ref, start, images, terms, total)
    if final:

        @pl.when(flag_ref[0] == 1)
        def _():
            edge = 2048 - last_ref.shape[-1]
            pool_terms(pairs_ref, last_ref, last_ref, edge, images, terms, total)

    power[...] = (
        total[pl.ds(32 * count, 128)] + total[pl.ds(half + 32 * count, 128)]
    ).reshape(8, 16, 128) * (1.0 / 64.0)
    for p in range(count):
        first, second = pairs_ref[p, 0], pairs_ref[p, 1]
        scale = lax.rsqrt((power[first] + 1e-6) * (power[second] + 1e-6)) * (1.0 / 64.0)
        re = (total[pl.ds(16 * p, 16)] + total[pl.ds(half + 16 * p, 16)]) * scale
        at = 16 * (count + p)
        im = (total[pl.ds(at, 16)] + total[pl.ds(half + at, 16)]) * scale
        for ref in extra:
            re, im = re + ref[0, p], im + ref[1, p]
        gamma_ref[0, p] = re
        gamma_ref[1, p] = im
        if final:
            coherence_ref[p] = jnp.sqrt(re * re + im * im)
    for copy in copies:
        copy.wait()


def looks(pairs, own, following, start, name, last=None, extra=(), tables=()):
    count = pairs.shape[0]
    rows = 16 * (2 * count + 8)
    vmem = pl.BlockSpec(memory_space=pltpu.VMEM)
    smem = pl.BlockSpec(memory_space=pltpu.SMEM)
    final = last is not None
    shapes = [jax.ShapeDtypeStruct((2, count, 16, 128), F32)]
    if final:
        shapes.append(jax.ShapeDtypeStruct((count, 16, 128), F32))
    shapes += [jax.ShapeDtypeStruct(table.shape, table.dtype) for table in tables]
    scratch = [
        pltpu.VMEM((2, 8, 2, 2, 64, 128), F32),
        pltpu.VMEM((2, 2 * rows, 256), BF16),
        pltpu.VMEM((2 * rows, 128), F32),
        pltpu.VMEM((8, 16, 128), F32),
    ]
    if tables:
        scratch.append(pltpu.SemaphoreType.DMA((len(tables),)))
    return pl.pallas_call(
        functools.partial(
            looks_kernel, start=start, tables=len(tables), added=len(extra), final=final
        ),
        out_shape=shapes,
        in_specs=[smem, vmem, vmem]
        + ([smem, vmem] if final else [])
        + [vmem] * len(extra)
        + [pl.BlockSpec(memory_space=pl.ANY)] * len(tables),
        out_specs=[vmem] * len(shapes),
        scratch_shapes=scratch,
        compiler_params=pltpu.CompilerParams(vmem_limit_bytes=12 << 20),
        name=name,
    )(pairs, own, following, *(last or ()), *extra, *tables)


def ring(power, axis, step, index):
    size = power.shape[axis]
    near = pltpu.roll(power, 1 if step > 0 else size - 1, axis)
    wrap = pltpu.roll(power, size - 31 if step > 0 else 31, axis)
    return jnp.where(index == (0 if step > 0 else 31), wrap, near)


def filter_kernel(
    odd_ref, near_ref, own_ref, far_ref, rows_ref, final_ref, fore_ref, back_ref,
    out_ref, field, spectra, weighted, result, fore, back,
):
    count = own_ref.shape[1]
    odd = 32 * odd_ref[0]
    for p in range(count):
        lanes = pl.ds(128 * p, 128)
        for part in range(2):
            for place, ref in ((32 - odd, near_ref), (16, own_ref), (odd, far_ref)):
                high, low = split(ref[part, p])
                at = pl.multiple_of(48 * part + place, 16)
                field[pl.ds(at, 16), lanes] = high
                field[pl.ds(96 + at, 16), lanes] = low
                field[pl.ds(192 + at, 16), lanes] = high
    across = lax.broadcasted_iota(jnp.int32, (128, 128), 0)
    along = lax.broadcasted_iota(jnp.int32, (128, 128), 1)
    for level in range(2):
        cosine = jnp.concatenate([fore_ref[level].astype(F32)] * 4, axis=0)
        sine = jnp.concatenate([fore_ref[2 + level].astype(F32)] * 4, axis=0)
        for block in range(BLOCKS):
            patch = 4 * block + (along >> 5) - (across >> 4)
            inside = (patch >= 0) & (patch <= 1) & (4 * block + (along >> 5) < PATCHES)
            cos, sin = (jnp.where(inside, value, 0.0) for value in (cosine, sine))
            at = 256 * block
            fore[level, pl.ds(0, 128), pl.ds(at, 128)] = cos.astype(BF16)
            fore[level, pl.ds(128, 128), pl.ds(at, 128)] = sin.astype(BF16)
            fore[level, pl.ds(0, 128), pl.ds(at + 128, 128)] = (-sin).astype(BF16)
            fore[level, pl.ds(128, 128), pl.ds(at + 128, 128)] = cos.astype(BF16)
    column = jnp.dot(rows_ref[...], field[...], preferred_element_type=F32)
    for p in range(count):
        for part in range(2):
            high, low = split(column[64 * part : 64 * part + 64, 128 * p : 128 * p + 128])
            spectra[0, pl.ds(64 * p, 64), pl.ds(128 * part, 128)] = high
            spectra[1, pl.ds(64 * p, 64), pl.ds(128 * part, 128)] = low
    for level in range(2):
        cosine, sine = back_ref[level].astype(F32), back_ref[2 + level].astype(F32)
        for block in range(BLOCKS):
            patch = 4 * block + (across >> 5) - (along >> 4)
            inside = (patch >= 0) & (patch <= 1) & (4 * block + (across >> 5) < PATCHES)
            cos, sin = (jnp.where(inside, value, 0.0) for value in (cosine, sine))
            at = 256 * block
            back[level, pl.ds(at, 128), pl.ds(0, 128)] = cos.astype(BF16)
            back[level, pl.ds(at, 128), pl.ds(128, 128)] = sin.astype(BF16)
            back[level, pl.ds(at + 128, 128), pl.ds(0, 128)] = (-sin).astype(BF16)
            back[level, pl.ds(at + 128, 128), pl.ds(128, 128)] = cos.astype(BF16)
    lane = lax.broadcasted_iota(jnp.int32, (64, 128), 1) & 31
    line = lax.broadcasted_iota(jnp.int32, (64, 128), 0) & 31
    for block in range(BLOCKS):
        at = pl.ds(256 * block, 256)
        both = (
            jnp.dot(spectra[0], fore[0, :, at], preferred_element_type=F32)
            + jnp.dot(spectra[1], fore[0, :, at], preferred_element_type=F32)
            + jnp.dot(spectra[0], fore[1, :, at], preferred_element_type=F32)
        )
        for p in range(count):
            re, im = both[64 * p : 64 * p + 64, :128], both[64 * p : 64 * p + 64, 128:]
            power = re * re + im * im
            power = power + ring(power, 1, 1, lane) + ring(power, 1, -1, lane)
            power = power + ring(power, 0, 1, line) + ring(power, 0, -1, line)
            weight = lax.rsqrt(lax.rsqrt(power * (1.0 / 9.0) + 1e-6))
            for part, value in enumerate((re, im)):
                high, low = split(value * weight)
                at = pl.ds(256 * block + 128 * part, 128)
                weighted[0, pl.ds(64 * p, 64), at] = high
                weighted[1, pl.ds(64 * p, 64), at] = low
    filtered = (
        jnp.dot(weighted[0], back[0], preferred_element_type=F32)
        + jnp.dot(weighted[1], back[0], preferred_element_type=F32)
        + jnp.dot(weighted[0], back[1], preferred_element_type=F32)
    )
    for p in range(count):
        lanes = pl.ds(128 * p, 128)
        for part in range(2):
            high, low = split(filtered[64 * p : 64 * p + 64, 128 * part : 128 * part + 128])
            at = 64 * part
            result[pl.ds(at, 64), lanes] = high
            result[pl.ds(128 + at, 64), lanes] = low
            result[pl.ds(256 + at, 64), lanes] = high
    out = jnp.dot(final_ref[...], result[...], preferred_element_type=F32)
    for p in range(count):
        for part in range(2):
            out_ref[part, p] = out[16 * part : 16 * part + 16, 128 * p : 128 * p + 128]


def goldstein(odd, near, own, far):
    count = own.shape[1]
    vmem = pl.BlockSpec(memory_space=pltpu.VMEM)
    tables = [jnp.asarray(table) for table in filter_tables()]
    return pl.pallas_call(
        filter_kernel,
        out_shape=jax.ShapeDtypeStruct((2, count, 16, 128), F32),
        in_specs=[pl.BlockSpec(memory_space=pltpu.SMEM)] + [vmem] * (3 + len(tables)),
        out_specs=vmem,
        scratch_shapes=[
            pltpu.VMEM((288, 128 * count), BF16),
            pltpu.VMEM((2, 64 * count, 256), BF16),
            pltpu.VMEM((2, 64 * count, 256 * BLOCKS), BF16),
            pltpu.VMEM((384, 128 * count), BF16),
            pltpu.VMEM((2, 256, 256 * BLOCKS), BF16),
            pltpu.VMEM((2, 256 * BLOCKS, 256), BF16),
        ],
        compiler_params=pltpu.CompilerParams(vmem_limit_bytes=16 << 20),
        name="goldstein",
    )(odd, near, own, far, *tables)


def shifted(value, axis, step):
    size = lax.axis_size(axis)
    return lax.ppermute(value, axis, [(i, i + step) for i in range(size) if 0 <= i + step < size])


def turned(value, axis, step):
    size = lax.axis_size(axis)
    return lax.ppermute(value, axis, [(i, (i + step) % size) for i in range(size)])


def swapped(value, axis, first):
    size = lax.axis_size(axis)
    pairs = [(i, i + 1) for i in range(first, size - 1, 2)]
    return lax.ppermute(value, axis, pairs + [(j, i) for i, j in pairs])


COLUMNS = (1024, 512)


def after(value, *done):
    return lax.optimization_barrier((value, *done))[0]


def per_device(slc, pairs):
    dates = slc.shape[1]
    block = lax.axis_index("date")
    here = pairs - block * dates
    edge = sum(COLUMNS)
    ends = np.cumsum((0, *COLUMNS))
    own = [slc[..., at : at + width] for at, width in zip(ends, COLUMNS)]
    own_last = slc[..., edge:]
    following = [turned(piece, "date", -1) for piece in own]
    previous_last = shifted(own_last, "date", 1)
    there = shifted(here, "date", 1)
    there = jnp.clip(there, 0, 2 * dates - 1)
    parts = []
    if False:
        parts += looks(here, own[0], following[0], 0, "looks_part")
        there = after(there, parts[0])
    [last_part] = looks(there, previous_last, own_last, edge, "looks_last")
    returned = shifted(last_part, "date", -1)
    here = after(here, last_part)
    for k in range(len(parts), len(COLUMNS) - 1):
        parts += looks(here, own[k], following[k], int(ends[k]), "looks_part")
    is_last = (block == lax.axis_size("date") - 1).astype(jnp.int32).reshape(1)
    gamma, coherence = looks(
        here, own[-1], following[-1], int(ends[-2]), "looks_end",
        last=(is_last, own_last), extra=(*parts, returned),
    )
    near = swapped(gamma, "space", 0)
    far = swapped(gamma, "space", 1)
    odd = (lax.axis_index("space") % 2).astype(jnp.int32).reshape(1)
    return coherence, goldstein(odd, near, gamma, far)


def solution(mesh):
    return jax.shard_map(
        per_device,
        mesh=mesh,
        in_specs=(P(None, "date", "space", None), P("date", None)),
        out_specs=(P("date", "space", None), P(None, "date", "space", None)),
        check_vma=False,
    )
```

```python
import functools

import jax
import jax.numpy as jnp
import numpy as np
from jax import lax
from jax.experimental import pallas as pl
from jax.experimental.pallas import tpu as pltpu
from jax.sharding import PartitionSpec as P

F32, BF16 = jnp.float32, jnp.bfloat16
PATCHES, BLOCKS = 9, 3


def split(value):
    high = value.astype(BF16)
    return high, (value - high.astype(F32)).astype(BF16)


def split_table(table):
    high = table.astype(np.float32).astype(jnp.bfloat16)
    low = (table - high.astype(np.float64)).astype(np.float32).astype(jnp.bfloat16)
    return high, low


@functools.cache
def filter_tables():
    index = np.arange(32)
    phase = 2.0 * np.pi * np.outer(index, index) / 32.0
    cosine, sine = np.cos(phase), np.sin(phase)
    taper = np.where(index < 16, (index + 0.5) / 16.0, (31.5 - index) / 16.0)
    rows = np.zeros((2, 2, 32, 2, 48))
    final = np.zeros((2, 16, 2, 2, 32))
    for j in range(2):
        at = slice(16 * j, 16 * j + 32)
        rows[0, j, :, 0, at], rows[0, j, :, 1, at] = cosine, sine
        rows[1, j, :, 0, at], rows[1, j, :, 1, at] = -sine, cosine
        for row in range(16):
            a = row + 16 * (1 - j)
            scale = taper[a] / 32.0
            final[0, row, 0, j], final[0, row, 1, j] = cosine[:, a] * scale, -sine[:, a] * scale
            final[1, row, 0, j], final[1, row, 1, j] = sine[:, a] * scale, cosine[:, a] * scale
    rows_high, rows_low = split_table(rows.reshape(128, 96))
    final_high, final_low = split_table(final.reshape(32, 128))
    lane = np.arange(128)
    place = (np.arange(32)[:, None] + 16 - 16 * (lane // 32)[None]) % 32
    fore = 2.0 * np.pi * place * (lane % 32)[None] / 32.0
    place = (lane[None] + 16 - 16 * (lane // 32)[:, None]) % 32
    back = 2.0 * np.pi * place * (lane % 32)[:, None] / 32.0
    scale = taper[place] / 32.0
    return (
        np.concatenate([rows_high, rows_high, rows_low], axis=1),
        np.concatenate([final_high, final_high, final_low], axis=1),
        np.stack([*split_table(np.cos(fore)), *split_table(np.sin(fore))]),
        np.stack([*split_table(np.cos(back) * scale), *split_table(np.sin(back) * scale)]),
    )


def pool_terms(pairs_ref, own_ref, next_ref, start, images, terms, total):
    count = pairs_ref.shape[0]
    half = terms.shape[1] // 2
    for c in range(own_ref.shape[-1] // 256):
        slot = c % 2
        for date in range(4):
            for part in range(2):
                for side in range(2):
                    at = pl.ds(256 * c + 128 * side, 128)
                    images[slot, date, part, side] = own_ref[part, date, :, at].astype(F32)
                    images[slot, 4 + date, part, side] = next_ref[part, date, :, at].astype(F32)

        def load(date, part, side, phase):
            return images[slot, date, part, side, pl.ds(phase, 16, stride=4), :]

        def keep(index, side, value):
            high, low = split(value)
            at = pl.ds(128 * side, 128)
            terms[slot, pl.ds(16 * index, 16), at] = high
            terms[slot, pl.ds(half + 16 * index, 16), at] = low

        for p in range(count):
            first, second = pairs_ref[p, 0], pairs_ref[p, 1]
            for side in range(2):
                re = im = None
                for phase in range(4):
                    ar, ai = load(first, 0, side, phase), load(first, 1, side, phase)
                    br, bi = load(second, 0, side, phase), load(second, 1, side, phase)
                    one, other = ar * br + ai * bi, ai * br - ar * bi
                    re, im = (one, other) if re is None else (re + one, im + other)
                keep(p, side, re)
                keep(count + p, side, im)
        for date in range(8):
            for side in range(2):
                square = None
                for phase in range(4):
                    re, im = load(date, 0, side, phase), load(date, 1, side, phase)
                    one = re * re + im * im
                    square = one if square is None else square + one
                keep(2 * count + date, side, square)
        sample = lax.broadcasted_iota(jnp.int32, (256, 128), 0)
        column = lax.broadcasted_iota(jnp.int32, (256, 128), 1)
        pool = ((sample >> 4) + (start // 16 + 16 * c) == column).astype(F32).astype(BF16)
        total[...] += jnp.dot(terms[slot], pool, preferred_element_type=F32)


def fetch(sources, targets, sems):
    return [
        pltpu.make_async_copy(source, target, sems.at[i])
        for i, (source, target) in enumerate(zip(sources, targets))
    ]


def looks_kernel(*refs, start, tables, added, final):
    take = iter(refs)
    pairs_ref, own_ref, next_ref = (next(take) for _ in range(3))
    flag_ref, last_ref = (next(take), next(take)) if final else (None, None)
    extra = [next(take) for _ in range(added)]
    sources = [next(take) for _ in range(tables)]
    gamma_ref = next(take)
    coherence_ref = next(take) if final else None
    targets = [next(take) for _ in range(tables)]
    images, terms, total, power = (next(take) for _ in range(4))
    copies = fetch(sources, targets, next(take)) if tables else []
    for copy in copies:
        copy.start()
    count = pairs_ref.shape[0]
    half = terms.shape[1] // 2
    total[...] = jnp.zeros_like(total)
    pool_terms(pairs_ref, own_ref, next_ref, start, images, terms, total)
    if final:

        @pl.when(flag_ref[0] == 1)
        def _():
            edge = 2048 - last_ref.shape[-1]
            pool_terms(pairs_ref, last_ref, last_ref, edge, images, terms, total)

    power[...] = (
        total[pl.ds(32 * count, 128)] + total[pl.ds(half + 32 * count, 128)]
    ).reshape(8, 16, 128) * (1.0 / 64.0)
    for p in range(count):
        first, second = pairs_ref[p, 0], pairs_ref[p, 1]
        scale = lax.rsqrt((power[first] + 1e-6) * (power[second] + 1e-6)) * (1.0 / 64.0)
        re = (total[pl.ds(16 * p, 16)] + total[pl.ds(half + 16 * p, 16)]) * scale
        at = 16 * (count + p)
        im = (total[pl.ds(at, 16)] + total[pl.ds(half + at, 16)]) * scale
        for ref in extra:
            re, im = re + ref[0, p], im + ref[1, p]
        gamma_ref[0, p] = re
        gamma_ref[1, p] = im
        if final:
            coherence_ref[p] = jnp.sqrt(re * re + im * im)
    for copy in copies:
        copy.wait()


def looks(pairs, own, following, start, name, last=None, extra=(), tables=()):
    count = pairs.shape[0]
    rows = 16 * (2 * count + 8)
    vmem = pl.BlockSpec(memory_space=pltpu.VMEM)
    smem = pl.BlockSpec(memory_space=pltpu.SMEM)
    final = last is not None
    shapes = [jax.ShapeDtypeStruct((2, count, 16, 128), F32)]
    if final:
        shapes.append(jax.ShapeDtypeStruct((count, 16, 128), F32))
    shapes += [jax.ShapeDtypeStruct(table.shape, table.dtype) for table in tables]
    scratch = [
        pltpu.VMEM((2, 8, 2, 2, 64, 128), F32),
        pltpu.VMEM((2, 2 * rows, 256), BF16),
        pltpu.VMEM((2 * rows, 128), F32),
        pltpu.VMEM((8, 16, 128), F32),
    ]
    if tables:
        scratch.append(pltpu.SemaphoreType.DMA((len(tables),)))
    return pl.pallas_call(
        functools.partial(
            looks_kernel, start=start, tables=len(tables), added=len(extra), final=final
        ),
        out_shape=shapes,
        in_specs=[smem, vmem, vmem]
        + ([smem, vmem] if final else [])
        + [vmem] * len(extra)
        + [pl.BlockSpec(memory_space=pl.ANY)] * len(tables),
        out_specs=[vmem] * len(shapes),
        scratch_shapes=scratch,
        compiler_params=pltpu.CompilerParams(vmem_limit_bytes=12 << 20),
        name=name,
    )(pairs, own, following, *(last or ()), *extra, *tables)


def ring(power, axis, step, index):
    size = power.shape[axis]
    near = pltpu.roll(power, 1 if step > 0 else size - 1, axis)
    wrap = pltpu.roll(power, size - 31 if step > 0 else 31, axis)
    return jnp.where(index == (0 if step > 0 else 31), wrap, near)


def filter_kernel(
    high_ref, own_ref, low_ref, rows_ref, final_ref, fore_ref, back_ref,
    out_ref, field, spectra, weighted, result, fore, back,
):
    count = own_ref.shape[1]
    for p in range(count):
        lanes = pl.ds(128 * p, 128)
        for part in range(2):
            for k, ref in enumerate((low_ref, own_ref, high_ref)):
                high, low = split(ref[part, p])
                at = 48 * part + 16 * k
                field[pl.ds(at, 16), lanes] = high
                field[pl.ds(96 + at, 16), lanes] = low
                field[pl.ds(192 + at, 16), lanes] = high
    across = lax.broadcasted_iota(jnp.int32, (128, 128), 0)
    along = lax.broadcasted_iota(jnp.int32, (128, 128), 1)
    for level in range(2):
        cosine = jnp.concatenate([fore_ref[level].astype(F32)] * 4, axis=0)
        sine = jnp.concatenate([fore_ref[2 + level].astype(F32)] * 4, axis=0)
        for block in range(BLOCKS):
            patch = 4 * block + (along >> 5) - (across >> 4)
            inside = (patch >= 0) & (patch <= 1) & (4 * block + (along >> 5) < PATCHES)
            cos, sin = (jnp.where(inside, value, 0.0) for value in (cosine, sine))
            at = 256 * block
            fore[level, pl.ds(0, 128), pl.ds(at, 128)] = cos.astype(BF16)
            fore[level, pl.ds(128, 128), pl.ds(at, 128)] = sin.astype(BF16)
            fore[level, pl.ds(0, 128), pl.ds(at + 128, 128)] = (-sin).astype(BF16)
            fore[level, pl.ds(128, 128), pl.ds(at + 128, 128)] = cos.astype(BF16)
    column = jnp.dot(rows_ref[...], field[...], preferred_element_type=F32)
    for p in range(count):
        for part in range(2):
            high, low = split(column[64 * part : 64 * part + 64, 128 * p : 128 * p + 128])
            spectra[0, pl.ds(64 * p, 64), pl.ds(128 * part, 128)] = high
            spectra[1, pl.ds(64 * p, 64), pl.ds(128 * part, 128)] = low
    for level in range(2):
        cosine, sine = back_ref[level].astype(F32), back_ref[2 + level].astype(F32)
        for block in range(BLOCKS):
            patch = 4 * block + (across >> 5) - (along >> 4)
            inside = (patch >= 0) & (patch <= 1) & (4 * block + (across >> 5) < PATCHES)
            cos, sin = (jnp.where(inside, value, 0.0) for value in (cosine, sine))
            at = 256 * block
            back[level, pl.ds(at, 128), pl.ds(0, 128)] = cos.astype(BF16)
            back[level, pl.ds(at, 128), pl.ds(128, 128)] = sin.astype(BF16)
            back[level, pl.ds(at + 128, 128), pl.ds(0, 128)] = (-sin).astype(BF16)
            back[level, pl.ds(at + 128, 128), pl.ds(128, 128)] = cos.astype(BF16)
    lane = lax.broadcasted_iota(jnp.int32, (64, 128), 1) & 31
    line = lax.broadcasted_iota(jnp.int32, (64, 128), 0) & 31
    for block in range(BLOCKS):
        at = pl.ds(256 * block, 256)
        both = (
            jnp.dot(spectra[0], fore[0, :, at], preferred_element_type=F32)
            + jnp.dot(spectra[1], fore[0, :, at], preferred_element_type=F32)
            + jnp.dot(spectra[0], fore[1, :, at], preferred_element_type=F32)
        )
        for p in range(count):
            re, im = both[64 * p : 64 * p + 64, :128], both[64 * p : 64 * p + 64, 128:]
            power = re * re + im * im
            power = power + ring(power, 1, 1, lane) + ring(power, 1, -1, lane)
            power = power + ring(power, 0, 1, line) + ring(power, 0, -1, line)
            weight = lax.rsqrt(lax.rsqrt(power * (1.0 / 9.0) + 1e-6))
            for part, value in enumerate((re, im)):
                high, low = split(value * weight)
                at = pl.ds(256 * block + 128 * part, 128)
                weighted[0, pl.ds(64 * p, 64), at] = high
                weighted[1, pl.ds(64 * p, 64), at] = low
    filtered = (
        jnp.dot(weighted[0], back[0], preferred_element_type=F32)
        + jnp.dot(weighted[1], back[0], preferred_element_type=F32)
        + jnp.dot(weighted[0], back[1], preferred_element_type=F32)
    )
    for p in range(count):
        lanes = pl.ds(128 * p, 128)
        for part in range(2):
            high, low = split(filtered[64 * p : 64 * p + 64, 128 * part : 128 * part + 128])
            at = 64 * part
            result[pl.ds(at, 64), lanes] = high
            result[pl.ds(128 + at, 64), lanes] = low
            result[pl.ds(256 + at, 64), lanes] = high
    out = jnp.dot(final_ref[...], result[...], preferred_element_type=F32)
    for p in range(count):
        for part in range(2):
            out_ref[part, p] = out[16 * part : 16 * part + 16, 128 * p : 128 * p + 128]


def goldstein(high, own, low):
    count = own.shape[1]
    vmem = pl.BlockSpec(memory_space=pltpu.VMEM)
    tables = [jnp.asarray(table) for table in filter_tables()]
    return pl.pallas_call(
        filter_kernel,
        out_shape=jax.ShapeDtypeStruct((2, count, 16, 128), F32),
        in_specs=[vmem] * (3 + len(tables)),
        out_specs=vmem,
        scratch_shapes=[
            pltpu.VMEM((288, 128 * count), BF16),
            pltpu.VMEM((2, 64 * count, 256), BF16),
            pltpu.VMEM((2, 64 * count, 256 * BLOCKS), BF16),
            pltpu.VMEM((384, 128 * count), BF16),
            pltpu.VMEM((2, 256, 256 * BLOCKS), BF16),
            pltpu.VMEM((2, 256 * BLOCKS, 256), BF16),
        ],
        compiler_params=pltpu.CompilerParams(vmem_limit_bytes=16 << 20),
        name="goldstein",
    )(high, own, low, *tables)


def shifted(value, axis, step):
    size = lax.axis_size(axis)
    return lax.ppermute(value, axis, [(i, i + step) for i in range(size) if 0 <= i + step < size])


def turned(value, axis, step):
    size = lax.axis_size(axis)
    return lax.ppermute(value, axis, [(i, (i + step) % size) for i in range(size)])


COLUMNS = (1024, 512)


def after(value, *done):
    return lax.optimization_barrier((value, *done))[0]


def per_device(slc, pairs):
    dates = slc.shape[1]
    block = lax.axis_index("date")
    here = pairs - block * dates
    edge = sum(COLUMNS)
    ends = np.cumsum((0, *COLUMNS))
    own = [slc[..., at : at + width] for at, width in zip(ends, COLUMNS)]
    own_last = slc[..., edge:]
    following = [turned(piece, "date", -1) for piece in own]
    previous_last = shifted(own_last, "date", 1)
    there = shifted(here, "date", 1)
    there = jnp.clip(there, 0, 2 * dates - 1)
    parts = []
    if False:
        parts += looks(here, own[0], following[0], 0, "looks_part")
        there = after(there, parts[0])
    [last_part] = looks(there, previous_last, own_last, edge, "looks_last")
    returned = shifted(last_part, "date", -1)
    here = after(here, last_part)
    for k in range(len(parts), len(COLUMNS) - 1):
        parts += looks(here, own[k], following[k], int(ends[k]), "looks_part")
    is_last = (block == lax.axis_size("date") - 1).astype(jnp.int32).reshape(1)
    gamma, coherence = looks(
        here, own[-1], following[-1], int(ends[-2]), "looks_end",
        last=(is_last, own_last), extra=(*parts, returned),
    )
    strip, strips = lax.axis_index("space"), lax.axis_size("space")
    low = jnp.where(strip == 0, 0.0, turned(gamma, "space", 1))
    high = jnp.where(strip == strips - 1, 0.0, turned(gamma, "space", -1))
    return coherence, goldstein(high, gamma, low)


def solution(mesh):
    return jax.shard_map(
        per_device,
        mesh=mesh,
        in_specs=(P(None, "date", "space", None), P("date", None)),
        out_specs=(P("date", "space", None), P(None, "date", "space", None)),
        check_vma=False,
    )
```

```python
import functools

import jax
import jax.numpy as jnp
import numpy as np
from jax import lax
from jax.experimental import pallas as pl
from jax.experimental.pallas import tpu as pltpu
from jax.sharding import PartitionSpec as P

F32, BF16 = jnp.float32, jnp.bfloat16
PATCHES, BLOCKS = 9, 3


def split(value):
    high = value.astype(BF16)
    return high, (value - high.astype(F32)).astype(BF16)


def split_table(table):
    high = table.astype(np.float32).astype(jnp.bfloat16)
    low = (table - high.astype(np.float64)).astype(np.float32).astype(jnp.bfloat16)
    return high, low


@functools.cache
def filter_tables():
    index = np.arange(32)
    phase = 2.0 * np.pi * np.outer(index, index) / 32.0
    cosine, sine = np.cos(phase), np.sin(phase)
    taper = np.where(index < 16, (index + 0.5) / 16.0, (31.5 - index) / 16.0)
    rows = np.zeros((2, 2, 32, 2, 48))
    final = np.zeros((2, 16, 2, 2, 32))
    for j in range(2):
        at = slice(16 * j, 16 * j + 32)
        rows[0, j, :, 0, at], rows[0, j, :, 1, at] = cosine, sine
        rows[1, j, :, 0, at], rows[1, j, :, 1, at] = -sine, cosine
        for row in range(16):
            a = row + 16 * (1 - j)
            scale = taper[a] / 32.0
            final[0, row, 0, j], final[0, row, 1, j] = cosine[:, a] * scale, -sine[:, a] * scale
            final[1, row, 0, j], final[1, row, 1, j] = sine[:, a] * scale, cosine[:, a] * scale
    rows_high, rows_low = split_table(rows.reshape(128, 96))
    final_high, final_low = split_table(final.reshape(32, 128))
    lane = np.arange(128)
    place = (np.arange(32)[:, None] + 16 - 16 * (lane // 32)[None]) % 32
    fore = 2.0 * np.pi * place * (lane % 32)[None] / 32.0
    place = (lane[None] + 16 - 16 * (lane // 32)[:, None]) % 32
    back = 2.0 * np.pi * place * (lane % 32)[:, None] / 32.0
    scale = taper[place] / 32.0
    return (
        np.concatenate([rows_high, rows_high, rows_low], axis=1),
        np.concatenate([final_high, final_high, final_low], axis=1),
        np.stack([*split_table(np.cos(fore)), *split_table(np.sin(fore))]),
        np.stack([*split_table(np.cos(back) * scale), *split_table(np.sin(back) * scale)]),
    )


def pool_terms(pairs_ref, own_ref, next_ref, start, images, terms, total):
    count = pairs_ref.shape[0]
    half = terms.shape[1] // 2
    for c in range(own_ref.shape[-1] // 256):
        slot = c % 2
        for date in range(4):
            for part in range(2):
                for side in range(2):
                    at = pl.ds(256 * c + 128 * side, 128)
                    images[slot, date, part, side] = own_ref[part, date, :, at].astype(F32)
                    images[slot, 4 + date, part, side] = next_ref[part, date, :, at].astype(F32)

        def load(date, part, side, phase):
            return images[slot, date, part, side, pl.ds(phase, 16, stride=4), :]

        def keep(index, side, value):
            high, low = split(value)
            at = pl.ds(128 * side, 128)
            terms[slot, pl.ds(16 * index, 16), at] = high
            terms[slot, pl.ds(half + 16 * index, 16), at] = low

        for p in range(count):
            first, second = pairs_ref[p, 0], pairs_ref[p, 1]
            for side in range(2):
                re = im = None
                for phase in range(4):
                    ar, ai = load(first, 0, side, phase), load(first, 1, side, phase)
                    br, bi = load(second, 0, side, phase), load(second, 1, side, phase)
                    one, other = ar * br + ai * bi, ai * br - ar * bi
                    re, im = (one, other) if re is None else (re + one, im + other)
                keep(p, side, re)
                keep(count + p, side, im)
        for date in range(8):
            for side in range(2):
                square = None
                for phase in range(4):
                    re, im = load(date, 0, side, phase), load(date, 1, side, phase)
                    one = re * re + im * im
                    square = one if square is None else square + one
                keep(2 * count + date, side, square)
        sample = lax.broadcasted_iota(jnp.int32, (256, 128), 0)
        column = lax.broadcasted_iota(jnp.int32, (256, 128), 1)
        pool = ((sample >> 4) + (start // 16 + 16 * c) == column).astype(F32).astype(BF16)
        total[...] += jnp.dot(terms[slot], pool, preferred_element_type=F32)


def fetch(sources, targets, sems):
    return [
        pltpu.make_async_copy(source, target, sems.at[i])
        for i, (source, target) in enumerate(zip(sources, targets))
    ]


def looks_kernel(*refs, start, tables, added, final):
    take = iter(refs)
    pairs_ref, own_ref, next_ref = (next(take) for _ in range(3))
    flag_ref, last_ref = (next(take), next(take)) if final else (None, None)
    extra = [next(take) for _ in range(added)]
    sources = [next(take) for _ in range(tables)]
    gamma_ref = next(take)
    coherence_ref = next(take) if final else None
    targets = [next(take) for _ in range(tables)]
    images, terms, total, power = (next(take) for _ in range(4))
    copies = fetch(sources, targets, next(take)) if tables else []
    for copy in copies:
        copy.start()
    count = pairs_ref.shape[0]
    half = terms.shape[1] // 2
    total[...] = jnp.zeros_like(total)
    pool_terms(pairs_ref, own_ref, next_ref, start, images, terms, total)
    if final:

        @pl.when(flag_ref[0] == 1)
        def _():
            edge = 2048 - last_ref.shape[-1]
            pool_terms(pairs_ref, last_ref, last_ref, edge, images, terms, total)

    power[...] = (
        total[pl.ds(32 * count, 128)] + total[pl.ds(half + 32 * count, 128)]
    ).reshape(8, 16, 128) * (1.0 / 64.0)
    for p in range(count):
        first, second = pairs_ref[p, 0], pairs_ref[p, 1]
        scale = lax.rsqrt((power[first] + 1e-6) * (power[second] + 1e-6)) * (1.0 / 64.0)
        re = (total[pl.ds(16 * p, 16)] + total[pl.ds(half + 16 * p, 16)]) * scale
        at = 16 * (count + p)
        im = (total[pl.ds(at, 16)] + total[pl.ds(half + at, 16)]) * scale
        for ref in extra:
            re, im = re + ref[0, p], im + ref[1, p]
        gamma_ref[0, p] = re
        gamma_ref[1, p] = im
        if final:
            coherence_ref[p] = jnp.sqrt(re * re + im * im)
    for copy in copies:
        copy.wait()


def looks(pairs, own, following, start, name, last=None, extra=(), tables=()):
    count = pairs.shape[0]
    rows = 16 * (2 * count + 8)
    vmem = pl.BlockSpec(memory_space=pltpu.VMEM)
    smem = pl.BlockSpec(memory_space=pltpu.SMEM)
    final = last is not None
    shapes = [jax.ShapeDtypeStruct((2, count, 16, 128), F32)]
    if final:
        shapes.append(jax.ShapeDtypeStruct((count, 16, 128), F32))
    shapes += [jax.ShapeDtypeStruct(table.shape, table.dtype) for table in tables]
    scratch = [
        pltpu.VMEM((2, 8, 2, 2, 64, 128), F32),
        pltpu.VMEM((2, 2 * rows, 256), BF16),
        pltpu.VMEM((2 * rows, 128), F32),
        pltpu.VMEM((8, 16, 128), F32),
    ]
    if tables:
        scratch.append(pltpu.SemaphoreType.DMA((len(tables),)))
    return pl.pallas_call(
        functools.partial(
            looks_kernel, start=start, tables=len(tables), added=len(extra), final=final
        ),
        out_shape=shapes,
        in_specs=[smem, vmem, vmem]
        + ([smem, vmem] if final else [])
        + [vmem] * len(extra)
        + [pl.BlockSpec(memory_space=pl.ANY)] * len(tables),
        out_specs=[vmem] * len(shapes),
        scratch_shapes=scratch,
        compiler_params=pltpu.CompilerParams(vmem_limit_bytes=12 << 20),
        name=name,
    )(pairs, own, following, *(last or ()), *extra, *tables)


def ring(power, axis, step, index):
    size = power.shape[axis]
    near = pltpu.roll(power, 1 if step > 0 else size - 1, axis)
    wrap = pltpu.roll(power, size - 31 if step > 0 else 31, axis)
    return jnp.where(index == (0 if step > 0 else 31), wrap, near)


def filter_kernel(
    high_ref, own_ref, low_ref, rows_ref, final_ref, fore_ref, back_ref,
    out_ref, field, spectra, weighted, result, fore, back,
):
    count = own_ref.shape[1]
    for p in range(count):
        lanes = pl.ds(128 * p, 128)
        for part in range(2):
            for k, ref in enumerate((low_ref, own_ref, high_ref)):
                high, low = split(ref[part, p])
                at = 48 * part + 16 * k
                field[pl.ds(at, 16), lanes] = high
                field[pl.ds(96 + at, 16), lanes] = low
                field[pl.ds(192 + at, 16), lanes] = high
    across = lax.broadcasted_iota(jnp.int32, (128, 128), 0)
    along = lax.broadcasted_iota(jnp.int32, (128, 128), 1)
    for level in range(2):
        cosine = jnp.concatenate([fore_ref[level].astype(F32)] * 4, axis=0)
        sine = jnp.concatenate([fore_ref[2 + level].astype(F32)] * 4, axis=0)
        for block in range(BLOCKS):
            patch = 4 * block + (along >> 5) - (across >> 4)
            inside = (patch >= 0) & (patch <= 1) & (4 * block + (along >> 5) < PATCHES)
            cos, sin = (jnp.where(inside, value, 0.0) for value in (cosine, sine))
            at = 256 * block
            fore[level, pl.ds(0, 128), pl.ds(at, 128)] = cos.astype(BF16)
            fore[level, pl.ds(128, 128), pl.ds(at, 128)] = sin.astype(BF16)
            fore[level, pl.ds(0, 128), pl.ds(at + 128, 128)] = (-sin).astype(BF16)
            fore[level, pl.ds(128, 128), pl.ds(at + 128, 128)] = cos.astype(BF16)
    column = jnp.dot(rows_ref[...], field[...], preferred_element_type=F32)
    for p in range(count):
        for part in range(2):
            high, low = split(column[64 * part : 64 * part + 64, 128 * p : 128 * p + 128])
            spectra[0, pl.ds(64 * p, 64), pl.ds(128 * part, 128)] = high
            spectra[1, pl.ds(64 * p, 64), pl.ds(128 * part, 128)] = low
    for level in range(2):
        cosine, sine = back_ref[level].astype(F32), back_ref[2 + level].astype(F32)
        for block in range(BLOCKS):
            patch = 4 * block + (across >> 5) - (along >> 4)
            inside = (patch >= 0) & (patch <= 1) & (4 * block + (across >> 5) < PATCHES)
            cos, sin = (jnp.where(inside, value, 0.0) for value in (cosine, sine))
            at = 256 * block
            back[level, pl.ds(at, 128), pl.ds(0, 128)] = cos.astype(BF16)
            back[level, pl.ds(at, 128), pl.ds(128, 128)] = sin.astype(BF16)
            back[level, pl.ds(at + 128, 128), pl.ds(0, 128)] = (-sin).astype(BF16)
            back[level, pl.ds(at + 128, 128), pl.ds(128, 128)] = cos.astype(BF16)
    lane = lax.broadcasted_iota(jnp.int32, (64, 128), 1) & 31
    line = lax.broadcasted_iota(jnp.int32, (64, 128), 0) & 31
    for block in range(BLOCKS):
        at = pl.ds(256 * block, 256)
        both = (
            jnp.dot(spectra[0], fore[0, :, at], preferred_element_type=F32)
            + jnp.dot(spectra[1], fore[0, :, at], preferred_element_type=F32)
            + jnp.dot(spectra[0], fore[1, :, at], preferred_element_type=F32)
        )
        for p in range(count):
            re, im = both[64 * p : 64 * p + 64, :128], both[64 * p : 64 * p + 64, 128:]
            power = re * re + im * im
            power = power + ring(power, 1, 1, lane) + ring(power, 1, -1, lane)
            power = power + ring(power, 0, 1, line) + ring(power, 0, -1, line)
            weight = lax.rsqrt(lax.rsqrt(power * (1.0 / 9.0) + 1e-6))
            for part, value in enumerate((re, im)):
                high, low = split(value * weight)
                at = pl.ds(256 * block + 128 * part, 128)
                weighted[0, pl.ds(64 * p, 64), at] = high
                weighted[1, pl.ds(64 * p, 64), at] = low
    filtered = (
        jnp.dot(weighted[0], back[0], preferred_element_type=F32)
        + jnp.dot(weighted[1], back[0], preferred_element_type=F32)
        + jnp.dot(weighted[0], back[1], preferred_element_type=F32)
    )
    for p in range(count):
        lanes = pl.ds(128 * p, 128)
        for part in range(2):
            high, low = split(filtered[64 * p : 64 * p + 64, 128 * part : 128 * part + 128])
            at = 64 * part
            result[pl.ds(at, 64), lanes] = high
            result[pl.ds(128 + at, 64), lanes] = low
            result[pl.ds(256 + at, 64), lanes] = high
    out = jnp.dot(final_ref[...], result[...], preferred_element_type=F32)
    for p in range(count):
        for part in range(2):
            out_ref[part, p] = out[16 * part : 16 * part + 16, 128 * p : 128 * p + 128]


def goldstein(high, own, low):
    count = own.shape[1]
    vmem = pl.BlockSpec(memory_space=pltpu.VMEM)
    tables = [jnp.asarray(table) for table in filter_tables()]
    return pl.pallas_call(
        filter_kernel,
        out_shape=jax.ShapeDtypeStruct((2, count, 16, 128), F32),
        in_specs=[vmem] * (3 + len(tables)),
        out_specs=vmem,
        scratch_shapes=[
            pltpu.VMEM((288, 128 * count), BF16),
            pltpu.VMEM((2, 64 * count, 256), BF16),
            pltpu.VMEM((2, 64 * count, 256 * BLOCKS), BF16),
            pltpu.VMEM((384, 128 * count), BF16),
            pltpu.VMEM((2, 256, 256 * BLOCKS), BF16),
            pltpu.VMEM((2, 256 * BLOCKS, 256), BF16),
        ],
        compiler_params=pltpu.CompilerParams(vmem_limit_bytes=16 << 20),
        name="goldstein",
    )(high, own, low, *tables)


def shifted(value, axis, step):
    size = lax.axis_size(axis)
    return lax.ppermute(value, axis, [(i, i + step) for i in range(size) if 0 <= i + step < size])


def turned(value, axis, step):
    size = lax.axis_size(axis)
    return lax.ppermute(value, axis, [(i, (i + step) % size) for i in range(size)])


COLUMNS = (1280, 256)


def after(value, *done):
    return lax.optimization_barrier((value, *done))[0]


def per_device(slc, pairs):
    dates = slc.shape[1]
    block = lax.axis_index("date")
    here = pairs - block * dates
    edge = sum(COLUMNS)
    ends = np.cumsum((0, *COLUMNS))
    own = [slc[..., at : at + width] for at, width in zip(ends, COLUMNS)]
    own_last = slc[..., edge:]
    following = [turned(piece, "date", -1) for piece in own]
    previous_last = shifted(own_last, "date", 1)
    there = shifted(here, "date", 1)
    there = jnp.clip(there, 0, 2 * dates - 1)
    parts = []
    if False:
        parts += looks(here, own[0], following[0], 0, "looks_part")
        there = after(there, parts[0])
    [last_part] = looks(there, previous_last, own_last, edge, "looks_last")
    returned = shifted(last_part, "date", -1)
    here = after(here, last_part)
    for k in range(len(parts), len(COLUMNS) - 1):
        parts += looks(here, own[k], following[k], int(ends[k]), "looks_part")
    is_last = (block == lax.axis_size("date") - 1).astype(jnp.int32).reshape(1)
    gamma, coherence = looks(
        here, own[-1], following[-1], int(ends[-2]), "looks_end",
        last=(is_last, own_last), extra=(*parts, returned),
    )
    strip, strips = lax.axis_index("space"), lax.axis_size("space")
    low = jnp.where(strip == 0, 0.0, turned(gamma, "space", 1))
    high = jnp.where(strip == strips - 1, 0.0, turned(gamma, "space", -1))
    return coherence, goldstein(high, gamma, low)


def solution(mesh):
    return jax.shard_map(
        per_device,
        mesh=mesh,
        in_specs=(P(None, "date", "space", None), P("date", None)),
        out_specs=(P("date", "space", None), P(None, "date", "space", None)),
        check_vma=False,
    )
```

```python
import functools

import jax
import jax.numpy as jnp
import numpy as np
from jax import lax
from jax.experimental import pallas as pl
from jax.experimental.pallas import tpu as pltpu
from jax.sharding import PartitionSpec as P

F32, BF16 = jnp.float32, jnp.bfloat16
PATCHES, BLOCKS = 9, 3


def split(value):
    high = value.astype(BF16)
    return high, (value - high.astype(F32)).astype(BF16)


def split_table(table):
    high = table.astype(np.float32).astype(jnp.bfloat16)
    low = (table - high.astype(np.float64)).astype(np.float32).astype(jnp.bfloat16)
    return high, low


@functools.cache
def filter_tables():
    index = np.arange(32)
    phase = 2.0 * np.pi * np.outer(index, index) / 32.0
    cosine, sine = np.cos(phase), np.sin(phase)
    taper = np.where(index < 16, (index + 0.5) / 16.0, (31.5 - index) / 16.0)
    rows = np.zeros((2, 2, 32, 2, 48))
    final = np.zeros((2, 16, 2, 2, 32))
    for j in range(2):
        at = slice(16 * j, 16 * j + 32)
        rows[0, j, :, 0, at], rows[0, j, :, 1, at] = cosine, sine
        rows[1, j, :, 0, at], rows[1, j, :, 1, at] = -sine, cosine
        for row in range(16):
            a = row + 16 * (1 - j)
            scale = taper[a] / 32.0
            final[0, row, 0, j], final[0, row, 1, j] = cosine[:, a] * scale, -sine[:, a] * scale
            final[1, row, 0, j], final[1, row, 1, j] = sine[:, a] * scale, cosine[:, a] * scale
    rows_high, rows_low = split_table(rows.reshape(128, 96))
    final_high, final_low = split_table(final.reshape(32, 128))
    lane = np.arange(128)
    place = (np.arange(32)[:, None] + 16 - 16 * (lane // 32)[None]) % 32
    fore = 2.0 * np.pi * place * (lane % 32)[None] / 32.0
    place = (lane[None] + 16 - 16 * (lane // 32)[:, None]) % 32
    back = 2.0 * np.pi * place * (lane % 32)[:, None] / 32.0
    scale = taper[place] / 32.0
    return (
        np.concatenate([rows_high, rows_high, rows_low], axis=1),
        np.concatenate([final_high, final_high, final_low], axis=1),
        np.stack([*split_table(np.cos(fore)), *split_table(np.sin(fore))]),
        np.stack([*split_table(np.cos(back) * scale), *split_table(np.sin(back) * scale)]),
    )


def pool_terms(pairs_ref, own_ref, next_ref, start, images, terms, total):
    count = pairs_ref.shape[0]
    half = terms.shape[1] // 2
    for c in range(own_ref.shape[-1] // 256):
        slot = c % 2
        for date in range(4):
            for part in range(2):
                for side in range(2):
                    at = pl.ds(256 * c + 128 * side, 128)
                    images[slot, date, part, side] = own_ref[part, date, :, at].astype(F32)
                    images[slot, 4 + date, part, side] = next_ref[part, date, :, at].astype(F32)

        def load(date, part, side, phase):
            return images[slot, date, part, side, pl.ds(phase, 16, stride=4), :]

        def keep(index, side, value):
            high, low = split(value)
            at = pl.ds(128 * side, 128)
            terms[slot, pl.ds(16 * index, 16), at] = high
            terms[slot, pl.ds(half + 16 * index, 16), at] = low

        for p in range(count):
            first, second = pairs_ref[p, 0], pairs_ref[p, 1]
            for side in range(2):
                re = im = None
                for phase in range(4):
                    ar, ai = load(first, 0, side, phase), load(first, 1, side, phase)
                    br, bi = load(second, 0, side, phase), load(second, 1, side, phase)
                    one, other = ar * br + ai * bi, ai * br - ar * bi
                    re, im = (one, other) if re is None else (re + one, im + other)
                keep(p, side, re)
                keep(count + p, side, im)
        for date in range(8):
            for side in range(2):
                square = None
                for phase in range(4):
                    re, im = load(date, 0, side, phase), load(date, 1, side, phase)
                    one = re * re + im * im
                    square = one if square is None else square + one
                keep(2 * count + date, side, square)
        sample = lax.broadcasted_iota(jnp.int32, (256, 128), 0)
        column = lax.broadcasted_iota(jnp.int32, (256, 128), 1)
        pool = ((sample >> 4) + (start // 16 + 16 * c) == column).astype(F32).astype(BF16)
        total[...] += jnp.dot(terms[slot], pool, preferred_element_type=F32)


def fetch(sources, targets, sems):
    return [
        pltpu.make_async_copy(source, target, sems.at[i])
        for i, (source, target) in enumerate(zip(sources, targets))
    ]


def looks_kernel(*refs, start, tables, added, final):
    take = iter(refs)
    pairs_ref, own_ref, next_ref = (next(take) for _ in range(3))
    flag_ref, last_ref = (next(take), next(take)) if final else (None, None)
    extra = [next(take) for _ in range(added)]
    sources = [next(take) for _ in range(tables)]
    gamma_ref = next(take)
    coherence_ref = next(take) if final else None
    targets = [next(take) for _ in range(tables)]
    images, terms, total, power = (next(take) for _ in range(4))
    copies = fetch(sources, targets, next(take)) if tables else []
    for copy in copies:
        copy.start()
    count = pairs_ref.shape[0]
    half = terms.shape[1] // 2
    total[...] = jnp.zeros_like(total)
    pool_terms(pairs_ref, own_ref, next_ref, start, images, terms, total)
    if final:

        @pl.when(flag_ref[0] == 1)
        def _():
            edge = 2048 - last_ref.shape[-1]
            pool_terms(pairs_ref, last_ref, last_ref, edge, images, terms, total)

    power[...] = (
        total[pl.ds(32 * count, 128)] + total[pl.ds(half + 32 * count, 128)]
    ).reshape(8, 16, 128) * (1.0 / 64.0)
    for p in range(count):
        first, second = pairs_ref[p, 0], pairs_ref[p, 1]
        scale = lax.rsqrt((power[first] + 1e-6) * (power[second] + 1e-6)) * (1.0 / 64.0)
        re = (total[pl.ds(16 * p, 16)] + total[pl.ds(half + 16 * p, 16)]) * scale
        at = 16 * (count + p)
        im = (total[pl.ds(at, 16)] + total[pl.ds(half + at, 16)]) * scale
        for ref in extra:
            re, im = re + ref[0, p], im + ref[1, p]
        gamma_ref[0, p] = re
        gamma_ref[1, p] = im
        if final:
            coherence_ref[p] = jnp.sqrt(re * re + im * im)
    for copy in copies:
        copy.wait()


def looks(pairs, own, following, start, name, last=None, extra=(), tables=()):
    count = pairs.shape[0]
    rows = 16 * (2 * count + 8)
    vmem = pl.BlockSpec(memory_space=pltpu.VMEM)
    smem = pl.BlockSpec(memory_space=pltpu.SMEM)
    final = last is not None
    shapes = [jax.ShapeDtypeStruct((2, count, 16, 128), F32)]
    if final:
        shapes.append(jax.ShapeDtypeStruct((count, 16, 128), F32))
    shapes += [jax.ShapeDtypeStruct(table.shape, table.dtype) for table in tables]
    scratch = [
        pltpu.VMEM((2, 8, 2, 2, 64, 128), F32),
        pltpu.VMEM((2, 2 * rows, 256), BF16),
        pltpu.VMEM((2 * rows, 128), F32),
        pltpu.VMEM((8, 16, 128), F32),
    ]
    if tables:
        scratch.append(pltpu.SemaphoreType.DMA((len(tables),)))
    return pl.pallas_call(
        functools.partial(
            looks_kernel, start=start, tables=len(tables), added=len(extra), final=final
        ),
        out_shape=shapes,
        in_specs=[smem, vmem, vmem]
        + ([smem, vmem] if final else [])
        + [vmem] * len(extra)
        + [pl.BlockSpec(memory_space=pl.ANY)] * len(tables),
        out_specs=[vmem] * len(shapes),
        scratch_shapes=scratch,
        compiler_params=pltpu.CompilerParams(vmem_limit_bytes=12 << 20),
        name=name,
    )(pairs, own, following, *(last or ()), *extra, *tables)


def ring(power, axis, step, index):
    size = power.shape[axis]
    near = pltpu.roll(power, 1 if step > 0 else size - 1, axis)
    wrap = pltpu.roll(power, size - 31 if step > 0 else 31, axis)
    return jnp.where(index == (0 if step > 0 else 31), wrap, near)


def filter_kernel(
    high_ref, own_ref, low_ref, rows_ref, final_ref, fore_ref, back_ref,
    out_ref, field, spectra, weighted, result, fore, back,
):
    count = own_ref.shape[1]
    for p in range(count):
        lanes = pl.ds(128 * p, 128)
        for part in range(2):
            for k, ref in enumerate((low_ref, own_ref, high_ref)):
                high, low = split(ref[part, p])
                at = 48 * part + 16 * k
                field[pl.ds(at, 16), lanes] = high
                field[pl.ds(96 + at, 16), lanes] = low
                field[pl.ds(192 + at, 16), lanes] = high
    across = lax.broadcasted_iota(jnp.int32, (128, 128), 0)
    along = lax.broadcasted_iota(jnp.int32, (128, 128), 1)
    for level in range(2):
        cosine = jnp.concatenate([fore_ref[level].astype(F32)] * 4, axis=0)
        sine = jnp.concatenate([fore_ref[2 + level].astype(F32)] * 4, axis=0)
        for block in range(BLOCKS):
            patch = 4 * block + (along >> 5) - (across >> 4)
            inside = (patch >= 0) & (patch <= 1) & (4 * block + (along >> 5) < PATCHES)
            cos, sin = (jnp.where(inside, value, 0.0) for value in (cosine, sine))
            at = 256 * block
            fore[level, pl.ds(0, 128), pl.ds(at, 128)] = cos.astype(BF16)
            fore[level, pl.ds(128, 128), pl.ds(at, 128)] = sin.astype(BF16)
            fore[level, pl.ds(0, 128), pl.ds(at + 128, 128)] = (-sin).astype(BF16)
            fore[level, pl.ds(128, 128), pl.ds(at + 128, 128)] = cos.astype(BF16)
    column = jnp.dot(rows_ref[...], field[...], preferred_element_type=F32)
    for p in range(count):
        for part in range(2):
            high, low = split(column[64 * part : 64 * part + 64, 128 * p : 128 * p + 128])
            spectra[0, pl.ds(64 * p, 64), pl.ds(128 * part, 128)] = high
            spectra[1, pl.ds(64 * p, 64), pl.ds(128 * part, 128)] = low
    for level in range(2):
        cosine, sine = back_ref[level].astype(F32), back_ref[2 + level].astype(F32)
        for block in range(BLOCKS):
            patch = 4 * block + (across >> 5) - (along >> 4)
            inside = (patch >= 0) & (patch <= 1) & (4 * block + (across >> 5) < PATCHES)
            cos, sin = (jnp.where(inside, value, 0.0) for value in (cosine, sine))
            at = 256 * block
            back[level, pl.ds(at, 128), pl.ds(0, 128)] = cos.astype(BF16)
            back[level, pl.ds(at, 128), pl.ds(128, 128)] = sin.astype(BF16)
            back[level, pl.ds(at + 128, 128), pl.ds(0, 128)] = (-sin).astype(BF16)
            back[level, pl.ds(at + 128, 128), pl.ds(128, 128)] = cos.astype(BF16)
    lane = lax.broadcasted_iota(jnp.int32, (64, 128), 1) & 31
    line = lax.broadcasted_iota(jnp.int32, (64, 128), 0) & 31
    for block in range(BLOCKS):
        at = pl.ds(256 * block, 256)
        both = (
            jnp.dot(spectra[0], fore[0, :, at], preferred_element_type=F32)
            + jnp.dot(spectra[1], fore[0, :, at], preferred_element_type=F32)
            + jnp.dot(spectra[0], fore[1, :, at], preferred_element_type=F32)
        )
        for p in range(count):
            re, im = both[64 * p : 64 * p + 64, :128], both[64 * p : 64 * p + 64, 128:]
            power = re * re + im * im
            power = power + ring(power, 1, 1, lane) + ring(power, 1, -1, lane)
            power = power + ring(power, 0, 1, line) + ring(power, 0, -1, line)
            weight = lax.rsqrt(lax.rsqrt(power * (1.0 / 9.0) + 1e-6))
            for part, value in enumerate((re, im)):
                high, low = split(value * weight)
                at = pl.ds(256 * block + 128 * part, 128)
                weighted[0, pl.ds(64 * p, 64), at] = high
                weighted[1, pl.ds(64 * p, 64), at] = low
    filtered = (
        jnp.dot(weighted[0], back[0], preferred_element_type=F32)
        + jnp.dot(weighted[1], back[0], preferred_element_type=F32)
        + jnp.dot(weighted[0], back[1], preferred_element_type=F32)
    )
    for p in range(count):
        lanes = pl.ds(128 * p, 128)
        for part in range(2):
            high, low = split(filtered[64 * p : 64 * p + 64, 128 * part : 128 * part + 128])
            at = 64 * part
            result[pl.ds(at, 64), lanes] = high
            result[pl.ds(128 + at, 64), lanes] = low
            result[pl.ds(256 + at, 64), lanes] = high
    out = jnp.dot(final_ref[...], result[...], preferred_element_type=F32)
    for p in range(count):
        for part in range(2):
            out_ref[part, p] = out[16 * part : 16 * part + 16, 128 * p : 128 * p + 128]


def goldstein(high, own, low):
    count = own.shape[1]
    vmem = pl.BlockSpec(memory_space=pltpu.VMEM)
    tables = [jnp.asarray(table) for table in filter_tables()]
    return pl.pallas_call(
        filter_kernel,
        out_shape=jax.ShapeDtypeStruct((2, count, 16, 128), F32),
        in_specs=[vmem] * (3 + len(tables)),
        out_specs=vmem,
        scratch_shapes=[
            pltpu.VMEM((288, 128 * count), BF16),
            pltpu.VMEM((2, 64 * count, 256), BF16),
            pltpu.VMEM((2, 64 * count, 256 * BLOCKS), BF16),
            pltpu.VMEM((384, 128 * count), BF16),
            pltpu.VMEM((2, 256, 256 * BLOCKS), BF16),
            pltpu.VMEM((2, 256 * BLOCKS, 256), BF16),
        ],
        compiler_params=pltpu.CompilerParams(vmem_limit_bytes=16 << 20),
        name="goldstein",
    )(high, own, low, *tables)


def shifted(value, axis, step):
    size = lax.axis_size(axis)
    return lax.ppermute(value, axis, [(i, i + step) for i in range(size) if 0 <= i + step < size])


def turned(value, axis, step):
    size = lax.axis_size(axis)
    return lax.ppermute(value, axis, [(i, (i + step) % size) for i in range(size)])


COLUMNS = (768, 768)


def after(value, *done):
    return lax.optimization_barrier((value, *done))[0]


def per_device(slc, pairs):
    dates = slc.shape[1]
    block = lax.axis_index("date")
    here = pairs - block * dates
    edge = sum(COLUMNS)
    ends = np.cumsum((0, *COLUMNS))
    own = [slc[..., at : at + width] for at, width in zip(ends, COLUMNS)]
    own_last = slc[..., edge:]
    following = [turned(piece, "date", -1) for piece in own]
    previous_last = shifted(own_last, "date", 1)
    there = shifted(here, "date", 1)
    there = jnp.clip(there, 0, 2 * dates - 1)
    parts = []
    if False:
        parts += looks(here, own[0], following[0], 0, "looks_part")
        there = after(there, parts[0])
    [last_part] = looks(there, previous_last, own_last, edge, "looks_last")
    returned = shifted(last_part, "date", -1)
    here = after(here, last_part)
    for k in range(len(parts), len(COLUMNS) - 1):
        parts += looks(here, own[k], following[k], int(ends[k]), "looks_part")
    is_last = (block == lax.axis_size("date") - 1).astype(jnp.int32).reshape(1)
    gamma, coherence = looks(
        here, own[-1], following[-1], int(ends[-2]), "looks_end",
        last=(is_last, own_last), extra=(*parts, returned),
    )
    strip, strips = lax.axis_index("space"), lax.axis_size("space")
    low = jnp.where(strip == 0, 0.0, turned(gamma, "space", 1))
    high = jnp.where(strip == strips - 1, 0.0, turned(gamma, "space", -1))
    return coherence, goldstein(high, gamma, low)


def solution(mesh):
    return jax.shard_map(
        per_device,
        mesh=mesh,
        in_specs=(P(None, "date", "space", None), P("date", None)),
        out_specs=(P("date", "space", None), P(None, "date", "space", None)),
        check_vma=False,
    )
```
